128 devices in a mesh: sec: 8 (over z_hi, y), tile: 16 (over x, z_lo, core).
Axes of the slice: x: 4, y: 4, z: 4 (z_hi: 2, z_lo: 2; z = z_hi * 2 + z_lo), core: 2. Of those that a mesh axis runs over, the one named last changes fastest.
Arguments:
- patches: bfloat16 [8, 2048, 160, 160], P('sec', 'tile'), may hold values from -6 to 6
- counts: int32 [8, 16], P('sec', 'tile'), may hold values from 16 to 128, as said below
- peak_shifts: int32 [8, 2, 2048], P('sec', None, 'tile'), may hold values from -3 to 3
- mesh_prior: float32 [8, 16, 2, 128, 128], P('sec', 'tile'), may hold values from -6 to 6
Outputs:
- pair_flows: float32 [8, 2, 2048], P('sec', None, 'tile')
- displacement: float32 [8, 16, 2, 128, 128], P('sec', 'tile')
The draws below stay inside these ranges and needn't reach their ends.
Inputs may be any that keep to these rules, and one draw needn't show every extreme that they name: Slots 0 to counts - 1 of a tile are live. Some tile of every draw has all 128 slots live.
All inputs are finite; a program needn't handle non-finite values.
Results may differ from the reference program's by a relative error of at most 0.0014.
Values may be sent and summed in bfloat16 or wider, within the bound.
A program may use at most 192 MiB of HBM per device.

```python
import jax
import jax.numpy as jnp
from jax import lax

L = 160
PT = 128
PCOLS = 16
NR = 128
NC = 128
ITERS = 8
NSECT = 8
TILES = 16
TCOLS = 16
TROWS = 1


def draw_counts(key, part):
    first_key, second_key = jax.random.split(jax.random.fold_in(key, 11))
    ranks = jax.random.randint(first_key, (NSECT * TILES,), 0, 8)
    base_counts = PT // (1 + ranks)
    chosen = jax.random.randint(second_key, (), 0, NSECT * TILES)
    positions = jnp.arange(NSECT * TILES, dtype=jnp.int32)
    filled = jnp.where(positions == chosen, PT, base_counts)
    return filled.reshape(NSECT, TILES).astype(jnp.int32)


def plant(values, own_key, smallest, top_value):
    longest = values.shape.index(max(values.shape))
    spots = []
    for shift in (0, 1):
        where = [jax.random.randint(jax.random.fold_in(own_key, axis), (), 0, length) for axis, length in enumerate(values.shape)]
        where[longest] = (where[longest] + shift) % values.shape[longest]
        spots.append(tuple(where))
    return values.at[spots[0]].set(smallest).at[spots[1]].set(top_value)


def block_levels(stream_key, dims, cuts, low, high):
    loudness, own = 1.0, jax.random.fold_in(stream_key, 6)
    for axis_at, blocks in cuts:
        heights = jnp.exp(jax.random.uniform(jax.random.fold_in(own, axis_at), (blocks,), jnp.float32, low / len(cuts), high / len(cuts)))
        loudness = loudness * jnp.repeat(heights, dims[axis_at] // blocks).reshape([-1 if axis == axis_at else 1 for axis in range(len(dims))])
    return loudness


def normal_values(rng, shape, deviation, most, cuts=(), kind=jnp.bfloat16):
    array = deviation * jax.random.normal(rng, shape, jnp.float32)
    if cuts:
        array = array * block_levels(rng, shape, cuts, -0.22, 0.18)
    return jnp.clip(array, -most, most).astype(kind)


def setup_inputs(seed: int = 0) -> dict:
    streams_of = jax.random.split(jax.random.key(seed), 5)
    return {
        "patches": normal_values(streams_of[0], (NSECT, TILES * PT, L, L), 1.0, 6.0, ((0, 8), (1, 16))),
        "counts": draw_counts(jax.random.fold_in(streams_of[4], 71), 0),
        "peak_shifts": plant(jax.random.randint(streams_of[2], (NSECT, 2, TILES * PT), -3, 4), jax.random.fold_in(streams_of[2], 1), -3, 3).astype(jnp.int32),
        "mesh_prior": normal_values(streams_of[3], (NSECT, TILES, 2, NR, NC), 1.0, 6.0, ((0, 8), (1, 16)), jnp.float32),
    }


stiffness = 1.0
pull_weight = 4.0
relaxation = 0.8
highest = lax.Precision.HIGHEST


def dft_tables(extent):
    freq_index = jnp.arange(extent, dtype=jnp.int32)
    phases = (2.0 * jnp.pi / extent) * jnp.mod(freq_index[:, None] * freq_index[None, :], extent).astype(jnp.float32)
    cosine_part = jnp.cos(phases)
    sine_part = jnp.sin(phases)
    left_table = jnp.concatenate([cosine_part, sine_part], 0).astype(jnp.bfloat16)
    right_table = jnp.concatenate([cosine_part, -sine_part], 1).astype(jnp.bfloat16)
    return left_table, right_table


def spectra(images, left_table, right_table):
    extent = images.shape[-1]
    halfway = jnp.einsum("bmn,nk->bmk", images.astype(jnp.float32), right_table.astype(jnp.float32), precision=highest).astype(jnp.bfloat16)
    spectra_all = jnp.einsum("jm,bmk->bjk", left_table.astype(jnp.float32), halfway.astype(jnp.float32), precision=highest)
    real_part = spectra_all[:, :extent, :extent] + spectra_all[:, extent:, extent:]
    imag_part = spectra_all[:, :extent, extent:] - spectra_all[:, extent:, :extent]
    return real_part, imag_part


def window_flows(real_a, imag_a, real_b, imag_b, offsets):
    extent = real_a.shape[-1]
    cross_real = real_a * real_b + imag_a * imag_b
    cross_imag = real_a * imag_b - imag_a * real_b
    freq_index = jnp.arange(extent, dtype=jnp.int32)
    offsets_near = jnp.arange(3, dtype=jnp.int32) - 1

    def waves(shifts):
        lag_values = shifts[:, None] + offsets_near[None, :]
        phases = (2.0 * jnp.pi / extent) * jnp.mod(lag_values[:, :, None] * freq_index[None, None, :], extent).astype(jnp.float32)
        return jnp.cos(phases), jnp.sin(phases)

    row_cosine, row_sine = waves(offsets[0])
    col_cosine, col_sine = waves(offsets[1])
    inner_real = jnp.einsum("bkl,bcl->bkc", cross_real, col_cosine, precision=highest) - jnp.einsum("bkl,bcl->bkc", cross_imag, col_sine, precision=highest)
    inner_imag = jnp.einsum("bkl,bcl->bkc", cross_real, col_sine, precision=highest) + jnp.einsum("bkl,bcl->bkc", cross_imag, col_cosine, precision=highest)
    scores = (jnp.einsum("bak,bkc->bac", row_cosine, inner_real, precision=highest) - jnp.einsum("bak,bkc->bac", row_sine, inner_imag, precision=highest)) / float(extent) ** 3
    weights = scores * scores
    totals = 1.0 + jnp.sum(weights, axis=(1, 2))
    lag_float = offsets_near.astype(jnp.float32)
    shift_rows = jnp.sum(weights * lag_float[None, :, None], axis=(1, 2)) / totals
    shift_cols = jnp.sum(weights * lag_float[None, None, :], axis=(1, 2)) / totals
    return jnp.stack([offsets[0].astype(jnp.float32) + shift_rows, offsets[1].astype(jnp.float32) + shift_cols], 0)


def block_flows(current, following, offsets, left_table, right_table):
    group_size = current.shape[0]
    real_part, imag_part = spectra(jnp.concatenate([current, following], 0), left_table, right_table)
    return window_flows(real_part[:group_size], imag_part[:group_size], real_part[group_size:], imag_part[group_size:], offsets)


def tile_flows(current, following, offsets, live_count, left_table, right_table):
    slots = current.shape[0]
    group_size = 8

    def step(block_index, totals):
        start = (block_index * group_size).astype(jnp.int32)
        first = lax.dynamic_slice_in_dim(current, start, group_size, 0)
        second = lax.dynamic_slice_in_dim(following, start, group_size, 0)
        picked = lax.dynamic_slice_in_dim(offsets, start, group_size, 1)
        return lax.dynamic_update_slice_in_dim(totals, block_flows(first, second, picked, left_table, right_table), start, 1)

    count_blocks = (live_count + group_size - 1) // group_size
    totals = lax.fori_loop(0, count_blocks, step, jnp.zeros((2, slots), jnp.float32))
    live_mask = jnp.arange(slots, dtype=jnp.int32) < live_count
    return jnp.where(live_mask[None, :], totals, 0.0)


def spread_nodes(values, node_rows, node_cols):
    slots = values.shape[-1]
    patch_rows = slots // PCOLS
    leading = values.shape[:-1]
    shaped = values.reshape(leading + (patch_rows, 1, PCOLS, 1))
    widths = [(0, 0)] * len(leading) + [(0, 0), (0, node_rows // patch_rows - 1), (0, 0), (0, node_cols // PCOLS - 1)]
    return jnp.pad(shaped, widths).reshape(leading + (node_rows, node_cols))


def relax_update(moving, padded, target, weight):
    beside = padded[..., :-2, 1:-1] + padded[..., 2:, 1:-1] + padded[..., 1:-1, :-2] + padded[..., 1:-1, 2:]
    pulling = pull_weight * weight[..., None, :, :]
    return moving + relaxation * (stiffness * (beside - 4.0 * moving) + pulling * (target - moving)) / (4.0 * stiffness + pulling)


def to_grid(values):
    comps = values.shape[1]
    shaped = values.reshape(NSECT, TROWS, TCOLS, comps, NR, NC)
    return shaped.transpose(0, 3, 1, 4, 2, 5).reshape(NSECT, comps, TROWS * NR, TCOLS * NC)


def from_grid(values):
    comps = values.shape[1]
    shaped = values.reshape(NSECT, comps, TROWS, NR, TCOLS, NC)
    return shaped.transpose(0, 2, 4, 1, 3, 5).reshape(NSECT, TILES, comps, NR, NC)


def reference(patches, counts, peak_shifts, mesh_prior):
    left_table, right_table = dft_tables(L)
    following = jnp.concatenate([patches[1:], jnp.zeros_like(patches[:1])], 0)
    tile_total = NSECT * TILES
    current = patches.reshape(tile_total, PT, L, L)
    following = following.reshape(tile_total, PT, L, L)
    offsets = peak_shifts.reshape(NSECT, 2, TILES, PT).transpose(0, 2, 1, 3).reshape(tile_total, 2, PT)
    live_counts = counts.reshape(tile_total)

    def one_tile(packed):
        return tile_flows(packed[0], packed[1], packed[2], packed[3], left_table, right_table)

    flows_tiles = lax.map(one_tile, (current, following, offsets, live_counts))
    flows_out = flows_tiles.reshape(NSECT, TILES, 2, PT).transpose(0, 2, 1, 3).reshape(NSECT, 2, TILES * PT)
    live_mask = (jnp.arange(PT, dtype=jnp.int32)[None, :] < live_counts[:, None]).astype(jnp.float32)
    target = spread_nodes(flows_tiles, NR, NC)
    weight = spread_nodes(live_mask[:, None, :], NR, NC)
    moving = to_grid(mesh_prior.reshape(tile_total, 2, NR, NC))
    target_grid = to_grid(target)
    weight_grid = to_grid(weight)[:, 0]
    for sweep in range(ITERS):
        padded = jnp.pad(moving, ((0, 0), (0, 0), (1, 1), (1, 1)))
        moving = relax_update(moving, padded, target_grid, weight_grid)
    return flows_out, from_grid(moving)
```

```python
import functools

import jax
import jax.numpy as jnp
from jax import lax
from jax.experimental import pallas as pl
from jax.experimental.pallas import tpu as pltpu
from jax.sharding import PartitionSpec as P

PCOLS = 16
ITERS = 8
REACH = 4
GROUP = 4
CHUNKS = 4

highest = lax.Precision.HIGHEST


def moved(block, axis, distance):
    devices = range(lax.axis_size(axis))
    route = [(i - distance, i) for i in devices if i - distance in devices]
    return lax.ppermute(block, axis, route)


def shift_tables(extent, width):
    tail = extent - 128
    lane = jnp.arange(width, dtype=jnp.int32)
    column = jnp.where(lane < 128, lane, 128 + (lane - 128) % tail)
    shifts = jnp.arange(-REACH, REACH + 1, dtype=jnp.int32)
    source = jnp.mod(column[None, :] - shifts[:, None], extent)
    rows = jnp.arange(extent, dtype=jnp.int32)
    return (source[:, None, :] == rows[None, :, None]).astype(jnp.bfloat16)


def pack_group(images):
    extent = images[0].shape[0]
    tail = extent - 128
    row = lax.broadcasted_iota(jnp.int32, (tail, 128), 0)
    col = lax.broadcasted_iota(jnp.int32, (tail, 128), 1)
    joined = None
    for r, image in enumerate(images):
        spread = (col == row + tail * r).astype(jnp.bfloat16)
        part = jnp.dot(image[:, 128:], spread, preferred_element_type=jnp.float32)
        joined = part if joined is None else joined + part
    return [image[:, :128] for image in images] + [joined.astype(jnp.bfloat16)]


def pack_kernel(x_ref, o_ref):
    packed = pack_group([x_ref[r] for r in range(GROUP)])
    for i, piece in enumerate(packed):
        o_ref[0, i] = piece


def pack(patches, start, count):
    extent = patches.shape[-1]
    first = start // GROUP
    return pl.pallas_call(
        pack_kernel,
        grid=(count // GROUP,),
        in_specs=[
            pl.BlockSpec((None, GROUP, extent, extent), lambda i: (0, i + first, 0, 0))
        ],
        out_specs=pl.BlockSpec((1, GROUP + 1, extent, 128), lambda i: (i, 0, 0, 0)),
        out_shape=jax.ShapeDtypeStruct((count // GROUP, GROUP + 1, extent, 128), jnp.bfloat16),
        cost_estimate=pl.CostEstimate(
            flops=2 * count * extent * 32 * 128,
            bytes_accessed=count * extent * (256 + extent) * 2,
            transcendentals=0,
        ),
    )(patches)


def strips(extent):
    found = []
    for i in range(extent // 8):
        cols = {c % extent for c in range(8 * i - REACH, 8 * i + 8 + REACH)}
        found += [(i, t) for t in sorted({c // 128 for c in cols})]
    return found


def correlate(local, main, tails, r, p, q, table):
    extent = local.shape[0]
    tail = extent - 128
    lane = lax.broadcasted_iota(jnp.int32, (extent, 128), 1)
    own = jnp.where(lane // tail == r, tails.astype(jnp.float32), 0.0).astype(jnp.bfloat16)
    other = jnp.concatenate([main, own], 1)
    base = (
        lax.broadcasted_iota(jnp.int32, (8, 128), 1)
        - lax.broadcasted_iota(jnp.int32, (8, 128), 0)
        - p
    )
    products = []
    for b in range(3):
        variant = jnp.dot(
            local, table(q + b - 1 + REACH), preferred_element_type=jnp.float32
        ).astype(jnp.bfloat16)
        products.append(
            lax.dot_general(
                variant, other, (((1,), (1,)), ((), ())), preferred_element_type=jnp.float32
            )
        )
    sums = [[jnp.zeros((8, 128), jnp.float32) for _ in range(3)] for _ in range(3)]
    for i, t in strips(extent):
        for a in range(3):
            gap = base + (128 * t - 8 * i - (a - 1))
            hit = gap == 0
            if i == 0:
                hit = hit | (gap == extent)
            if i == extent // 8 - 1:
                hit = hit | (gap == -extent)
            for b in range(3):
                piece = products[b][8 * i : 8 * i + 8, 128 * t : min(128 * t + 128, extent)]
                if piece.shape[1] < 128:
                    piece = jnp.concatenate(
                        [piece, jnp.zeros((8, 128 - piece.shape[1]), jnp.float32)], 1
                    )
                sums[a][b] = sums[a][b] + jnp.where(hit, piece, 0.0)
    return [jnp.sum(sums[a][b], axis=0, keepdims=True) for a in range(3) for b in range(3)]


def fractions(rows, extent):
    ones = jnp.ones((8, 128), jnp.float32)
    weights = []
    for row in rows:
        score = lax.dot_general(
            ones, row, (((1,), (1,)), ((), ())), precision=highest, preferred_element_type=jnp.float32
        )[:1] / float(extent)
        weights.append(score * score)
    total = 1.0 + sum(weights)
    rows_part = (weights[6] + weights[7] + weights[8] - weights[0] - weights[1] - weights[2]) / total
    cols_part = (weights[2] + weights[5] + weights[8] - weights[0] - weights[3] - weights[6]) / total
    return rows_part, cols_part


def core_kernel(shift_ref, x_ref, y_ref, table_ref, o_ref, rows_ref):
    group = pl.program_id(0)
    extent = x_ref.shape[-1]
    for r in range(GROUP):
        slot = group * GROUP + r
        rows = correlate(
            x_ref[r],
            y_ref[0, r],
            y_ref[0, GROUP],
            r,
            shift_ref[0, slot],
            shift_ref[1, slot],
            lambda k: table_ref[k],
        )
        for k in range(9):
            rows_ref[k, pl.ds(slot, 1), :] = rows[k]

    @pl.when(group == pl.num_programs(0) - 1)
    def _():
        first, second = fractions([rows_ref[k] for k in range(9)], extent)
        o_ref[0:1, :] = first
        o_ref[1:2, :] = second


def core(patches, start, other, shifts, table):
    extent = patches.shape[-1]
    groups = other.shape[0]
    count = groups * GROUP
    first = start // GROUP
    return pl.pallas_call(
        core_kernel,
        grid_spec=pltpu.PrefetchScalarGridSpec(
            num_scalar_prefetch=1,
            grid=(groups,),
            in_specs=[
                pl.BlockSpec((None, GROUP, extent, extent), lambda i, _: (0, i + first, 0, 0)),
                pl.BlockSpec((1, GROUP + 1, extent, 128), lambda i, _: (i, 0, 0, 0)),
                pl.BlockSpec(table.shape, lambda i, _: (0, 0, 0)),
            ],
            out_specs=pl.BlockSpec((2, count), lambda i, _: (0, 0)),
            scratch_shapes=[pltpu.VMEM((9, count, 128), jnp.float32)],
        ),
        out_shape=jax.ShapeDtypeStruct((2, count), jnp.float32),
        cost_estimate=pl.CostEstimate(
            flops=2 * count * 3 * extent * 256 * 2 * extent,
            bytes_accessed=count * extent * (256 + extent) * 2,
            transcendentals=0,
        ),
    )(shifts, patches, other, table)


def node_fields(flows, live, edges, rows, cols):
    total = flows.shape[1]
    slots = total // 3
    patch_rows = slots // PCOLS
    step = cols // PCOLS
    slot = lax.broadcasted_iota(jnp.int32, (total, 2 * cols), 0)
    lane = lax.broadcasted_iota(jnp.int32, (total, 2 * cols), 1)
    part, within = slot // slots, slot % PCOLS
    home = jnp.where(
        part == 0,
        step * within,
        jnp.where(
            part == 1,
            jnp.where(within == 0, cols, -1),
            jnp.where(within == PCOLS - 1, 2 * cols - step, -1),
        ),
    )
    place = (lane == home).astype(jnp.float32)
    row_of = lax.broadcasted_iota(jnp.int32, (patch_rows, total), 1) % slots // PCOLS
    pick = row_of == lax.broadcasted_iota(jnp.int32, (patch_rows, total), 0)
    left = jnp.concatenate(
        [jnp.where(pick, line, 0.0) for line in (flows[0:1], flows[1:2], live)], 0
    )
    lines = jnp.dot(left, place, precision=highest, preferred_element_type=jnp.float32)
    spread = (
        lax.broadcasted_iota(jnp.int32, (rows, patch_rows), 0)
        == (rows // patch_rows) * lax.broadcasted_iota(jnp.int32, (rows, patch_rows), 1)
    ).astype(jnp.float32)
    return [
        jnp.dot(
            spread,
            lines[patch_rows * k : patch_rows * (k + 1)],
            precision=highest,
            preferred_element_type=jnp.float32,
        )
        for k in range(3)
    ]


def relax(fields, goals, weight, inside):
    rows = weight.shape[0]
    row = lax.broadcasted_iota(jnp.int32, weight.shape, 0)
    gain = (0.2 - 0.1 * weight) * inside
    goals = [0.4 * goal for goal in goals]
    for _ in range(ITERS):
        moved_fields = []
        for field, goal in zip(fields, goals):
            above = jnp.where(row == 0, 0.0, pltpu.roll(field, 1, 0))
            below = jnp.where(row == rows - 1, 0.0, pltpu.roll(field, rows - 1, 0))
            left = pltpu.roll(field, 1, 1)
            right = pltpu.roll(field, field.shape[1] - 1, 1)
            moved_fields.append(
                0.2 * field + gain * ((above + below) + (left + right)) + goal
            )
        fields = moved_fields
    return fields


def relax_kernel(edge_ref, prior_ref, flows_ref, live_ref, o_ref):
    rows, double = prior_ref.shape[1:]
    cols = double // 2
    goal_a, goal_b, weight = node_fields(flows_ref[...], live_ref[...], None, rows, cols)
    lane = lax.broadcasted_iota(jnp.int32, (rows, double), 1)
    west = jnp.where(edge_ref[0] == 1, 0.0, 1.0)
    east = jnp.where(edge_ref[1] == 1, 0.0, 1.0)
    inside = jnp.where(
        lane < cols, 1.0, jnp.where(lane < cols + ITERS, east, jnp.where(lane >= double - ITERS, west, 0.0))
    )
    done = relax([prior_ref[0], prior_ref[1]], [goal_a, goal_b], weight, inside)
    o_ref[0] = done[0][:, :cols]
    o_ref[1] = done[1][:, :cols]


def body(patches, counts, peak_shifts, mesh_prior):
    extent = patches.shape[-1]
    slots = patches.shape[1]
    half = slots // 2
    size = half // CHUNKS
    sec, tile = lax.axis_index("sec"), lax.axis_index("tile")
    shifts = peak_shifts[0]
    table = shift_tables(extent, 256)
    prior = mesh_prior[0, 0]
    cols = prior.shape[-1]

    down, up = [], []
    for c in range(CHUNKS):
        down.append(moved(pack(patches, c * size, size), "sec", -1))
        up.append(moved(pack(patches, half + c * size, size), "sec", 1))
    before = -moved(shifts, "sec", 1)
    west_prior = moved(prior[..., -ITERS:], "tile", 1)
    east_prior = moved(prior[..., :ITERS], "tile", -1)
    count_of = jnp.broadcast_to(counts, (1, slots))
    west_count, east_count = moved(count_of, "tile", 1), moved(count_of, "tile", -1)
    middle = jnp.zeros(prior.shape[:-1] + (cols - 2 * ITERS,), jnp.float32)
    wide = jnp.concatenate([prior, east_prior, middle, west_prior], -1)

    kept, given = [], []
    for c in range(CHUNKS):
        lo, hi = c * size, (c + 1) * size
        kept.append(core(patches, lo, down[c], shifts[:, lo:hi], table))
        given.append(core(patches, half + lo, up[c], before[:, half + lo : half + hi], table))
    back = moved(jnp.concatenate(given, -1), "sec", -1)
    fraction = jnp.concatenate(kept + [-back], -1)
    position = jnp.arange(slots, dtype=jnp.int32)[None, :]
    live = (position < count_of).astype(jnp.float32)
    flows = jnp.where(live > 0, shifts.astype(jnp.float32) + fraction, 0.0)
    west_flows, east_flows = moved(flows, "tile", 1), moved(flows, "tile", -1)
    west_live = (position < west_count).astype(jnp.float32)
    east_live = (position < east_count).astype(jnp.float32)
    last = lax.axis_size("tile") - 1
    edges = jnp.stack([tile == 0, tile == last]).astype(jnp.int32)
    displacement = pl.pallas_call(
        relax_kernel,
        in_specs=[pl.BlockSpec(memory_space=pltpu.SMEM)] + [pl.BlockSpec(memory_space=pltpu.VMEM)] * 3,
        out_specs=pl.BlockSpec(memory_space=pltpu.VMEM),
        out_shape=jax.ShapeDtypeStruct(prior.shape, jnp.float32),
    )(
        edges,
        wide,
        jnp.concatenate([flows, east_flows, west_flows], -1),
        jnp.concatenate([live, east_live, west_live], -1),
    )
    return flows[None], displacement[None, None]


def solution(mesh):
    placed = (
        P("sec", "tile", None, None),
        P("sec", "tile"),
        P("sec", None, "tile"),
        P("sec", "tile", None, None, None),
    )
    return jax.shard_map(
        body,
        mesh=mesh,
        in_specs=placed,
        out_specs=(P("sec", None, "tile"), P("sec", "tile", None, None, None)),
        check_vma=False,
    )
```

```python
import functools

import jax
import jax.numpy as jnp
from jax import lax
from jax.experimental import pallas as pl
from jax.experimental.pallas import tpu as pltpu
from jax.sharding import PartitionSpec as P

PCOLS = 16
ITERS = 8
REACH = 3
RIM = 8

highest = lax.Precision.HIGHEST
MESH = pl.DeviceIdType.MESH


def chunk_sizes(extent):
    size = max(REACH + 1, extent // 10)
    return [size] * (extent // 2 // size) + [REACH + 1]


def build_shifted(dst, local, temp, base, low, high, row_shift, col_shift):
    extent = local.shape[0]
    row_shift = jnp.broadcast_to(row_shift, (extent, row_shift.shape[1]))
    col_shift = jnp.broadcast_to(col_shift, (extent, col_shift.shape[1]))

    def row(i, carry):
        total = None
        for k in range(-REACH, REACH + 1):
            at = base + i + k
            value = local[lax.rem(at + extent, extent)].astype(jnp.float32)
            if low > 0:
                value = value * jnp.where((at >= low) & (at < high), 1.0, 0.0)
            total = value if total is None else jnp.where(row_shift == k, value, total)
        temp[pl.ds(RIM, extent), :] = total
        temp[pl.ds(0, RIM), :] = total[extent - RIM :]
        temp[pl.ds(RIM + extent, RIM), :] = total[:RIM]
        total = None
        for k in range(-REACH, REACH + 1):
            value = temp[pl.ds(RIM + k, extent), :]
            total = value if total is None else jnp.where(col_shift == k, value, total)
        dst[i, pl.ds(RIM, extent), :] = total
        dst[i, pl.ds(0, RIM), :] = total[extent - RIM :]
        dst[i, pl.ds(RIM + extent, RIM), :] = total[:RIM]
        return carry

    lax.fori_loop(0, dst.shape[0], row, 0)


def add_lags(sums, other, shifted, start, count):
    extent, lanes = other.shape[1:]

    def row(i, totals):
        r = start + i
        value = other[r].astype(jnp.float32)
        result = []
        for a in range(3):
            for b in range(3):
                product = value * shifted[r + a, pl.ds(RIM + b - 1, extent), :]
                total = totals[3 * a + b]
                for j in range(extent // 8):
                    total = total + product[8 * j : 8 * j + 8]
                result.append(total)
        return tuple(result)

    begun = tuple(sums[k] for k in range(9))
    for k, total in enumerate(lax.fori_loop(0, count, row, begun)):
        sums[k] = total


def node_fields(lines, rows, cols):
    total = lines[0].shape[1]
    slots = total // 3
    patch_rows = slots // PCOLS
    step = cols // PCOLS
    slot = lax.broadcasted_iota(jnp.int32, (total, 2 * cols), 0)
    lane = lax.broadcasted_iota(jnp.int32, (total, 2 * cols), 1)
    part, within = slot // slots, slot % PCOLS
    home = jnp.where(
        part == 0,
        step * within,
        jnp.where(
            part == 1,
            jnp.where(within == 0, cols, -1),
            jnp.where(within == PCOLS - 1, 2 * cols - step, -1),
        ),
    )
    place = (lane == home).astype(jnp.float32)
    row_of = lax.broadcasted_iota(jnp.int32, (patch_rows, total), 1) % slots // PCOLS
    pick = row_of == lax.broadcasted_iota(jnp.int32, (patch_rows, total), 0)
    left = jnp.concatenate([jnp.where(pick, line, 0.0) for line in lines], 0)
    spots = jnp.dot(left, place, precision=highest, preferred_element_type=jnp.float32)
    spread = (
        lax.broadcasted_iota(jnp.int32, (rows, patch_rows), 0)
        == (rows // patch_rows) * lax.broadcasted_iota(jnp.int32, (rows, patch_rows), 1)
    ).astype(jnp.float32)
    return [
        jnp.dot(
            spread,
            spots[patch_rows * k : patch_rows * (k + 1)],
            precision=highest,
            preferred_element_type=jnp.float32,
        )
        for k in range(len(lines))
    ]


def relax(fields, goals, gain):
    rows = gain.shape[0]
    row = lax.broadcasted_iota(jnp.int32, gain.shape, 0)
    for _ in range(ITERS):
        following = []
        for field, goal in zip(fields, goals):
            above = jnp.where(row == 0, 0.0, pltpu.roll(field, 1, 0))
            below = jnp.where(row == rows - 1, 0.0, pltpu.roll(field, rows - 1, 0))
            left = pltpu.roll(field, 1, 1)
            right = pltpu.roll(field, field.shape[1] - 1, 1)
            following.append(0.2 * field + gain * ((above + below) + (left + right)) + goal)
        fields = following
    return fields


def kernel(
    sections, tiles,
    patch_ref, count_ref, shift_ref, prior_ref,
    flow_ref, out_ref,
    local, from_above, from_below, shifted_up, shifted_down, temp,
    far_shift, far_prior, sums, part_out, part_in, state, far_state,
    local_sem, up_send, up_recv, down_send, down_recv,
    shift_sem, part_sem, prior_sem, state_sem,
):
    sec, tile = lax.axis_index("sec"), lax.axis_index("tile")
    extent, lanes = local.shape[1:]
    half = extent // 2
    upper = half + REACH + 1
    sizes = chunk_sizes(extent)
    has_below, has_above = sec > 0, sec < sections - 1
    has_west, has_east = tile > 0, tile < tiles - 1

    def when_each(pairs):
        for have, run in pairs:
            pl.when(have)(run)

    part_out[...] = jnp.zeros_like(part_out)
    part_in[...] = jnp.zeros_like(part_in)
    state[...] = jnp.zeros_like(state)
    far_state[...] = jnp.zeros_like(far_state)
    barrier = pltpu.get_barrier_semaphore()

    def greet(where):
        return lambda: pl.semaphore_signal(
            barrier, 1, device_id=where, device_id_type=MESH
        )

    when_each(
        [
            (has_below, greet({"sec": sec - 1})),
            (has_above, greet({"sec": sec + 1})),
            (has_west, greet({"tile": tile - 1})),
            (has_east, greet({"tile": tile + 1})),
        ]
    )
    mine = pltpu.make_async_copy(patch_ref, local, local_sem)
    mine.start()
    ends = (
        jnp.where(sec == 0, 1, 0)
        + jnp.where(sec == sections - 1, 1, 0)
        + jnp.where(tile == 0, 1, 0)
        + jnp.where(tile == tiles - 1, 1, 0)
    )
    pl.semaphore_wait(barrier, 4 - ends)

    def remote(src, dst, send, recv, where):
        return pltpu.make_async_remote_copy(
            src_ref=src,
            dst_ref=dst,
            send_sem=send,
            recv_sem=recv,
            device_id=where,
            device_id_type=MESH,
        )

    shift_copy = remote(
        shift_ref, far_shift, shift_sem.at[0], shift_sem.at[1], {"sec": sec + 1}
    )
    pl.when(has_above)(shift_copy.start)
    ups, downs = [], []
    at = 0
    for c, size in enumerate(sizes):
        rows = pl.ds(at, size)
        ups.append(
            remote(patch_ref.at[rows], from_below.at[rows], up_send.at[c], up_recv.at[c], {"sec": sec + 1})
        )
        source = pl.ds((half + at) % extent, size)
        downs.append(
            remote(patch_ref.at[source], from_above.at[rows], down_send.at[c], down_recv.at[c], {"sec": sec - 1})
        )
        pl.when(has_above)(ups[c].start)
        pl.when(has_below)(downs[c].start)
        at += size
    to_east = remote(prior_ref, far_prior.at[1], prior_sem.at[0], prior_sem.at[1], {"tile": tile + 1})
    to_west = remote(prior_ref, far_prior.at[0], prior_sem.at[2], prior_sem.at[3], {"tile": tile - 1})
    pl.when(has_east)(to_east.start)
    pl.when(has_west)(to_west.start)

    sums[...] = jnp.zeros_like(sums)
    mine.wait()

    @pl.when(has_above)
    def _():
        build_shifted(
            shifted_down, local, temp, half - 1, upper, extent, -shift_ref[0:1, :], -shift_ref[1:2, :]
        )
        shift_copy.wait_send()

    @pl.when(has_below)
    def _():
        shift_copy.wait_recv()
        build_shifted(
            shifted_up, local, temp, -1, 0, extent, far_shift[0:1, :], far_shift[1:2, :]
        )

    at = 0
    for c, size in enumerate(sizes):

        @pl.when(has_below)
        def _():
            ups[c].wait_recv()
            add_lags(sums.at[0], from_below, shifted_up, at, size)

        if c == len(sizes) - 1:

            @pl.when(has_below)
            def _():
                for k in range(9):
                    part_out[k : k + 1, :] = jnp.sum(sums[0, k], axis=0, keepdims=True)

        @pl.when(has_above)
        def _():
            downs[c].wait_recv()
            add_lags(sums.at[1], from_above, shifted_down, at, size)

        at += size

    part_copy = remote(part_out, part_in, part_sem.at[0], part_sem.at[1], {"sec": sec - 1})
    pl.when(has_below)(part_copy.start)
    pl.when(has_above)(part_copy.wait_recv)

    weights = []
    for k in range(9):
        score = jnp.sum(sums[1, 8 - k], axis=0, keepdims=True) + part_in[k : k + 1, :]
        score = score / float(extent)
        weights.append(score * score)
    total = 1.0 + sum(weights)
    row_part = (weights[6] + weights[7] + weights[8] - weights[0] - weights[1] - weights[2]) / total
    col_part = (weights[2] + weights[5] + weights[8] - weights[0] - weights[3] - weights[6]) / total
    live = lax.broadcasted_iota(jnp.int32, (1, lanes), 1) < count_ref[0, 0]
    flow_a = jnp.where(live, shift_ref[0:1, :].astype(jnp.float32) + row_part, 0.0)
    flow_b = jnp.where(live, shift_ref[1:2, :].astype(jnp.float32) + col_part, 0.0)
    alive = jnp.where(live, 1.0, 0.0)
    state[0:1, :] = flow_a
    state[1:2, :] = flow_b
    state[2:3, :] = alive
    state_east = remote(state, far_state.at[1], state_sem.at[0], state_sem.at[1], {"tile": tile + 1})
    state_west = remote(state, far_state.at[0], state_sem.at[2], state_sem.at[3], {"tile": tile - 1})
    pl.when(has_east)(state_east.start)
    pl.when(has_west)(state_west.start)
    flow_ref[0:1, :] = flow_a
    flow_ref[1:2, :] = flow_b

    pl.when(has_west)(to_east.wait_recv)
    pl.when(has_east)(to_west.wait_recv)
    rows, cols = prior_ref.shape[1:]
    lane = lax.broadcasted_iota(jnp.int32, (rows, cols), 1)
    in_east = (lane < ITERS) & has_east
    in_west = (lane >= cols - ITERS) & has_west
    fields = [
        jnp.concatenate(
            [
                prior_ref[k],
                jnp.where(in_east, far_prior[0, k], jnp.where(in_west, far_prior[1, k], 0.0)),
            ],
            1,
        )
        for k in range(2)
    ]
    inside = jnp.concatenate(
        [jnp.ones((rows, cols), jnp.float32), jnp.where(in_east | in_west, 1.0, 0.0)], 1
    )
    pl.when(has_west)(state_east.wait_recv)
    pl.when(has_east)(state_west.wait_recv)
    lines = [
        jnp.concatenate([mid, far_state[0, k : k + 1, :], far_state[1, k : k + 1, :]], 1)
        for k, mid in enumerate((flow_a, flow_b, alive))
    ]
    goal_a, goal_b, weight = node_fields(lines, rows, cols)
    gain = (0.2 - 0.1 * weight) * inside
    done = relax(fields, [0.4 * goal_a, 0.4 * goal_b], gain)
    out_ref[0] = done[0][:, :cols]
    out_ref[1] = done[1][:, :cols]

    for c in range(len(sizes)):
        pl.when(has_above)(ups[c].wait_send)
        pl.when(has_below)(downs[c].wait_send)
    pl.when(has_east)(to_east.wait_send)
    pl.when(has_west)(to_west.wait_send)
    pl.when(has_below)(part_copy.wait_send)
    pl.when(has_east)(state_east.wait_send)
    pl.when(has_west)(state_west.wait_send)


def body(patches, counts, peak_shifts, mesh_prior):
    sections, tiles = lax.axis_size("sec"), lax.axis_size("tile")
    by_slot = jnp.transpose(patches[0], (1, 2, 0))
    extent, _, slots = by_slot.shape
    prior = mesh_prior[0, 0]
    chunks = len(chunk_sizes(extent))
    sent = extent // 2 + REACH + 1
    wide = (sent + 2, extent + 2 * RIM, slots)
    sems = pltpu.SemaphoreType.DMA
    vmem = pl.BlockSpec(memory_space=pltpu.VMEM)
    flows, displacement = pl.pallas_call(
        functools.partial(kernel, sections, tiles),
        in_specs=[
            pl.BlockSpec(memory_space=pl.ANY),
            pl.BlockSpec(memory_space=pltpu.SMEM),
            vmem,
            vmem,
        ],
        out_specs=[vmem, vmem],
        out_shape=[
            jax.ShapeDtypeStruct((2, slots), jnp.float32),
            jax.ShapeDtypeStruct(prior.shape, jnp.float32),
        ],
        scratch_shapes=[
            pltpu.VMEM(by_slot.shape, jnp.bfloat16),
            pltpu.VMEM((sent, extent, slots), jnp.bfloat16),
            pltpu.VMEM((sent, extent, slots), jnp.bfloat16),
            pltpu.VMEM(wide, jnp.float32),
            pltpu.VMEM(wide, jnp.float32),
            pltpu.VMEM(wide[1:], jnp.float32),
            pltpu.VMEM((2, slots), jnp.int32),
            pltpu.VMEM((2,) + prior.shape, jnp.float32),
            pltpu.VMEM((2, 9, 8, slots), jnp.float32),
            pltpu.VMEM((16, slots), jnp.float32),
            pltpu.VMEM((16, slots), jnp.float32),
            pltpu.VMEM((8, slots), jnp.float32),
            pltpu.VMEM((2, 8, slots), jnp.float32),
            sems,
            sems((chunks,)),
            sems((chunks,)),
            sems((chunks,)),
            sems((chunks,)),
            sems((2,)),
            sems((2,)),
            sems((4,)),
            sems((4,)),
        ],
        compiler_params=pltpu.CompilerParams(collective_id=0, has_side_effects=True),
    )(by_slot, counts, peak_shifts[0], prior)
    return flows[None], displacement[None, None]


def solution(mesh):
    placed = (
        P("sec", "tile", None, None),
        P("sec", "tile"),
        P("sec", None, "tile"),
        P("sec", "tile", None, None, None),
    )
    return jax.shard_map(
        body,
        mesh=mesh,
        in_specs=placed,
        out_specs=(P("sec", None, "tile"), P("sec", "tile", None, None, None)),
        check_vma=False,
    )
```

```python
import functools

import jax
import jax.numpy as jnp
from jax import lax
from jax.experimental import pallas as pl
from jax.experimental.pallas import tpu as pltpu
from jax.sharding import PartitionSpec as P

PCOLS = 16
ITERS = 8
REACH = 3
RIM = 8

MESH = pl.DeviceIdType.MESH


def chunk_sizes(extent):
    half, size = extent // 2, max(6, extent // 10)
    full = half // size - 1
    up = [size] * full + [half - size * full - 4, 4]
    down = [size] * full + [half - size * full - 4, 2 * REACH]
    return up, down


def build_shifted(dst, local, temp, base, low, high, row_shift, col_shift):
    extent = local.shape[0]
    row_shift = jnp.broadcast_to(row_shift, (extent, row_shift.shape[1]))
    col_shift = jnp.broadcast_to(col_shift, (extent, col_shift.shape[1]))

    def row(i, carry):
        total = None
        for k in range(-REACH, REACH + 1):
            at = base + i + k
            value = local[lax.rem(at + extent, extent)].astype(jnp.float32)
            if low > 0:
                value = value * jnp.where((at >= low) & (at < high), 1.0, 0.0)
            total = value if total is None else jnp.where(row_shift == k, value, total)
        temp[pl.ds(RIM, extent), :] = total
        temp[pl.ds(0, RIM), :] = total[extent - RIM :]
        temp[pl.ds(RIM + extent, RIM), :] = total[:RIM]
        total = None
        for k in range(-REACH, REACH + 1):
            value = temp[pl.ds(RIM + k, extent), :]
            total = value if total is None else jnp.where(col_shift == k, value, total)
        dst[i, pl.ds(RIM, extent), :] = total
        dst[i, pl.ds(0, RIM), :] = total[extent - RIM :]
        dst[i, pl.ds(RIM + extent, RIM), :] = total[:RIM]
        return carry

    lax.fori_loop(0, dst.shape[0], row, 0)


def add_lags(sums, other, start, shifted, first, count):
    extent, lanes = other.shape[1:]

    def row(i, totals):
        value = other[start + i].astype(jnp.float32)
        result = []
        for a in range(3):
            for b in range(3):
                product = value * shifted[first + i + a, pl.ds(RIM + b - 1, extent), :]
                total = totals[3 * a + b]
                for j in range(extent // 8):
                    total = total + product[8 * j : 8 * j + 8]
                result.append(total)
        return tuple(result)

    begun = tuple(sums[k] for k in range(9))
    for k, total in enumerate(lax.fori_loop(0, count, row, begun)):
        sums[k] = total


def slot_places(extent_lanes, lanes, cols, patch_cols, homes):
    slot = lax.broadcasted_iota(jnp.int32, (2 * lanes, extent_lanes), 0)
    lane = lax.broadcasted_iota(jnp.int32, (2 * lanes, extent_lanes), 1)
    within = slot % patch_cols
    column = jnp.where(slot < lanes, within, jnp.where(within == 0, patch_cols, -1))
    return jnp.where(column == homes(lane), 1.0, 0.0).astype(jnp.bfloat16)


def by_patch_row(line, patch_rows):
    shape = (patch_rows, line.shape[1])
    slots = patch_rows * PCOLS
    of = lax.broadcasted_iota(jnp.int32, shape, 1) % slots // PCOLS
    return jnp.where(of == lax.broadcasted_iota(jnp.int32, shape, 0), line, 0.0)


def flow_lines(scores, row_shift, col_shift, live):
    weights = [score * score for score in scores]
    total = 1.0 + sum(weights)
    row_part = (weights[6] + weights[7] + weights[8] - weights[0] - weights[1] - weights[2]) / total
    col_part = (weights[2] + weights[5] + weights[8] - weights[0] - weights[3] - weights[6]) / total
    return (
        jnp.where(live > 0.0, row_shift + row_part, 0.0),
        jnp.where(live > 0.0, col_shift + col_part, 0.0),
    )


def kernel(
    sections, tiles,
    patch_ref, count_ref, shift_ref, prior_ref,
    flow_ref, out_ref,
    local, merged, from_above, from_below, shifted_up, shifted_down, shifted_rim, temp, sums,
    count, shift, far_shift, prior, far_prior, fields, goals, gain,
    info, east_info, part_up, part_down, own_up, east_up, east_down,
    local_sem, up_send, up_recv, down_send, down_recv,
    shift_sem, prior_sem, info_sem, part_sem,
):
    sec, tile = lax.axis_index("sec"), lax.axis_index("tile")
    extent, lanes = local.shape[1:]
    half = extent // 2
    rim = 2 * REACH
    low, high = half + REACH - 1, extent - REACH + 1
    up_sizes, down_sizes = chunk_sizes(extent)
    rows, cols = prior.shape[1:]
    patch_rows = lanes // PCOLS
    row_step, col_step = rows // patch_rows, cols // PCOLS
    has_below, has_above = sec > 0, sec < sections - 1
    has_west, has_east = tile > 0, tile < tiles - 1

    for buffer in (info, east_info, part_up, part_down, own_up, east_up, east_down):
        buffer[...] = jnp.zeros_like(buffer)

    barrier = pltpu.get_barrier_semaphore()
    below, above = {"sec": sec - 1}, {"sec": sec + 1}
    west, east = {"tile": tile - 1}, {"tile": tile + 1}
    below_west = {"sec": sec - 1, "tile": tile - 1}
    above_east = {"sec": sec + 1, "tile": tile + 1}
    partners = [
        (has_below, below),
        (has_above, above),
        (has_west, west),
        (has_east, east),
        (has_below & has_west, below_west),
        (has_above & has_east, above_east),
    ]

    def greet(where):
        return lambda: pl.semaphore_signal(
            barrier, 1, device_id=where, device_id_type=MESH
        )

    waits = 0
    for have, where in partners:
        pl.when(have)(greet(where))
        waits = waits + jnp.where(have, 1, 0)
    mine = [
        pltpu.make_async_copy(src, dst, local_sem.at[k])
        for k, (src, dst) in enumerate(
            ((shift_ref, shift), (count_ref, count), (patch_ref, local), (prior_ref, prior))
        )
    ]
    for copy in mine:
        copy.start()
    pl.semaphore_wait(barrier, waits)

    def remote(src, dst, sems, k, where):
        return pltpu.make_async_remote_copy(
            src_ref=src,
            dst_ref=dst,
            send_sem=sems[0].at[k],
            recv_sem=sems[1].at[k],
            device_id=where,
            device_id_type=MESH,
        )

    def remote_at(src, dst, sems, k, where):
        send, recv = sems.at[2 * k], sems.at[2 * k + 1]
        return pltpu.make_async_remote_copy(
            src_ref=src, dst_ref=dst, send_sem=send, recv_sem=recv, device_id=where, device_id_type=MESH
        )

    shift_copy = remote_at(shift_ref, far_shift, shift_sem, 0, above)
    pl.when(has_above)(shift_copy.start)
    ups, downs = [], []
    at = 0
    for c, size in enumerate(up_sizes):
        part = pl.ds(at, size)
        ups.append(remote(patch_ref.at[part], from_below.at[part], (up_send, up_recv), c, above))
        at += size
    at = 0
    for c, size in enumerate(down_sizes):
        part = pl.ds(at, size)
        source = merged if c == len(down_sizes) - 1 else patch_ref.at[pl.ds(low + at, size)]
        downs.append(remote(source, from_above.at[part], (down_send, down_recv), c, below))
        at += size
    for c in range(len(up_sizes)):
        pl.when(has_above)(ups[c].start)
        if c < len(down_sizes) - 1:
            pl.when(has_below)(downs[c].start)
    to_east = remote_at(prior_ref, far_prior.at[1], prior_sem, 0, east)
    to_west = remote_at(prior_ref, far_prior.at[0], prior_sem, 1, west)
    pl.when(has_east)(to_east.start)
    pl.when(has_west)(to_west.start)

    sums[...] = jnp.zeros_like(sums)
    for copy in mine:
        copy.wait()
    alive = jnp.where(
        lax.broadcasted_iota(jnp.int32, (1, lanes), 1) < count[0, 0], 1.0, 0.0
    )
    row_shift = shift[0:1, :].astype(jnp.float32)
    col_shift = shift[1:2, :].astype(jnp.float32)
    info[0:1, :] = row_shift
    info[1:2, :] = col_shift
    info[2:3, :] = alive

    @pl.when(has_below)
    def _():
        shift_copy.wait_recv()
        for j in range(rim):
            merged[j] = jnp.where(
                jnp.broadcast_to(far_shift[0:1, :], (extent, lanes)) <= j - REACH,
                local[half - REACH - 1 + j].astype(jnp.float32),
                local[(extent - REACH + 1 + j) % extent].astype(jnp.float32),
            ).astype(jnp.bfloat16)
        build_shifted(
            shifted_up, local, temp, -1, 0, extent, far_shift[0:1, :], far_shift[1:2, :]
        )
        downs[-1].start()

    info_copy = remote_at(info, east_info, info_sem, 0, west)
    pl.when(has_west)(info_copy.start)

    @pl.when(has_above)
    def _():
        build_shifted(
            shifted_down, local, temp, half - REACH - 2, half, extent, -shift[0:1, :], -shift[1:2, :]
        )
        for i in range(rim + 2):
            shifted_rim[i] = shifted_down[i] + shifted_down[half + 2 + i]

    pl.when(has_west)(to_east.wait_recv)
    pl.when(has_east)(to_west.wait_recv)
    pl.when(has_east)(info_copy.wait_recv)
    lane = lax.broadcasted_iota(jnp.int32, (rows, cols), 1)
    in_east = (lane < ITERS) & has_east
    in_west = (lane >= cols - ITERS) & has_west
    for k in range(2):
        fields[k, :, :cols] = prior[k]
        fields[k, :, cols:] = jnp.where(
            in_east, far_prior[0, k], jnp.where(in_west, far_prior[1, k], 0.0)
        )
        fields[2 + k] = jnp.zeros((rows, 2 * cols), jnp.float32)
    inside = jnp.concatenate(
        [jnp.ones((rows, cols), jnp.float32), jnp.where(in_east | in_west, 1.0, 0.0)], 1
    )
    at_nodes = slot_places(
        2 * cols, lanes, cols, PCOLS,
        lambda lane: jnp.where(lane % col_step == 0, lane // col_step, -2),
    )
    both_alive = jnp.concatenate([alive, east_info[2:3, :]], 1)
    spots = jnp.dot(
        by_patch_row(both_alive, patch_rows).astype(jnp.bfloat16),
        at_nodes,
        preferred_element_type=jnp.float32,
    ).astype(jnp.bfloat16)
    spread = jnp.where(
        lax.broadcasted_iota(jnp.int32, (rows, patch_rows), 0)
        == row_step * lax.broadcasted_iota(jnp.int32, (rows, patch_rows), 1),
        1.0,
        0.0,
    ).astype(jnp.bfloat16)
    weight = jnp.dot(spread, spots, preferred_element_type=jnp.float32)
    gain[...] = (0.2 - 0.1 * weight) * inside
    wide_lane = lax.broadcasted_iota(jnp.int32, weight.shape, 1)
    for k in range(2):
        goals[k] = jnp.where(wide_lane // col_step % 2 == k, 0.4 * weight, 0.0)
    row = lax.broadcasted_iota(jnp.int32, weight.shape, 0)

    def sweep(_, carry):
        for k in range(4):
            field = fields[k]
            upper = jnp.where(row == 0, 0.0, pltpu.roll(field, 1, 0))
            lower = jnp.where(row == rows - 1, 0.0, pltpu.roll(field, rows - 1, 0))
            left = pltpu.roll(field, 1, 1)
            right = pltpu.roll(field, 2 * cols - 1, 1)
            field = 0.2 * field + gain[...] * ((upper + lower) + (left + right))
            fields[k] = field + goals[k - 2] if k >= 2 else field
        return carry

    lax.fori_loop(0, ITERS, sweep, 0)
    owners = slot_places(
        2 * cols, lanes, cols, PCOLS,
        lambda lane: jnp.where(
            lane < cols,
            2 * ((lane + col_step) // (2 * col_step)),
            2 * ((lane - cols) // (2 * col_step)) + 1,
        ),
    )

    up_at = down_at = 0
    for c, (up_size, down_size) in enumerate(zip(up_sizes, down_sizes, strict=True)):
        final = c == len(up_sizes) - 1

        @pl.when(has_below)
        def _():
            ups[c].wait_recv()
            add_lags(sums.at[0], from_below, up_at, shifted_up, up_at, up_size)

        if final:

            @pl.when(has_below)
            def _():
                for k in range(9):
                    part_up[k : k + 1, :] = jnp.sum(sums[0, k], axis=0, keepdims=True)

            up_part = remote_at(part_up, own_up, part_sem, 0, below)
            up_part_west = remote_at(part_up, east_up, part_sem, 1, below_west)
            pl.when(has_below)(up_part.start)
            pl.when(has_below & has_west)(up_part_west.start)

        @pl.when(has_above)
        def _():
            downs[c].wait_recv()
            if final:
                add_lags(sums.at[1], from_above, down_at, shifted_rim, 0, down_size)
            else:
                add_lags(sums.at[1], from_above, down_at, shifted_down, down_at + rim, down_size)

        up_at += up_size
        down_at += down_size

    for k in range(9):
        part_down[k : k + 1, :] = jnp.sum(sums[1, 8 - k], axis=0, keepdims=True)
    down_part = remote_at(part_down, east_down, part_sem, 2, west)
    pl.when(has_west)(down_part.start)

    pl.when(has_above)(up_part.wait_recv)
    scale = float(extent)
    flow_a, flow_b = flow_lines(
        [(part_down[k : k + 1, :] + own_up[k : k + 1, :]) / scale for k in range(9)],
        row_shift,
        col_shift,
        alive,
    )
    flow_ref[0:1, :] = flow_a
    flow_ref[1:2, :] = flow_b
    pl.when(has_east)(down_part.wait_recv)
    pl.when(has_above & has_east)(up_part_west.wait_recv)
    east_a, east_b = flow_lines(
        [(east_down[k : k + 1, :] + east_up[k : k + 1, :]) / scale for k in range(9)],
        east_info[0:1, :],
        east_info[1:2, :],
        east_info[2:3, :],
    )
    left = jnp.concatenate(
        [
            by_patch_row(jnp.concatenate([flow_a, east_a], 1), patch_rows),
            by_patch_row(jnp.concatenate([flow_b, east_b], 1), patch_rows),
        ],
        0,
    )
    first = left.astype(jnp.bfloat16)
    rest = left - first.astype(jnp.float32)
    second = rest.astype(jnp.bfloat16)
    third = (rest - second.astype(jnp.float32)).astype(jnp.bfloat16)
    values = sum(
        jnp.dot(piece, owners, preferred_element_type=jnp.float32)
        for piece in (first, second, third)
    )
    strip = row_step // 2
    for m in range(rows // strip):
        owner = (m + 1) // 2
        part = pl.ds(m * strip, strip)
        for k in range(2):
            result = fields[k, part, :cols]
            if owner < patch_rows:
                value = values[k * patch_rows + owner : k * patch_rows + owner + 1]
                result = (
                    result
                    + fields[2, part, :cols] * value[:, :cols]
                    + fields[3, part, :cols] * value[:, cols:]
                )
            out_ref[k, part, :] = result

    pl.when(has_above)(shift_copy.wait_send)
    for copy in ups:
        pl.when(has_above)(copy.wait_send)
    for copy in downs:
        pl.when(has_below)(copy.wait_send)
    pl.when(has_east)(to_east.wait_send)
    pl.when(has_west)(to_west.wait_send)
    pl.when(has_west)(info_copy.wait_send)
    pl.when(has_below)(up_part.wait_send)
    pl.when(has_below & has_west)(up_part_west.wait_send)
    pl.when(has_west)(down_part.wait_send)


def body(patches, counts, peak_shifts, mesh_prior):
    sections, tiles = lax.axis_size("sec"), lax.axis_size("tile")
    by_slot = jnp.transpose(patches[0], (1, 2, 0))
    extent, _, slots = by_slot.shape
    prior = mesh_prior[0, 0]
    rows, cols = prior.shape[1:]
    half, rim = extent // 2, 2 * REACH
    up_sizes, down_sizes = chunk_sizes(extent)
    padded = extent + 2 * RIM
    sems = pltpu.SemaphoreType.DMA
    vmem = pl.BlockSpec(memory_space=pltpu.VMEM)
    f32, bf16 = jnp.float32, jnp.bfloat16
    flows, displacement = pl.pallas_call(
        functools.partial(kernel, sections, tiles),
        in_specs=[pl.BlockSpec(memory_space=pl.ANY)] * 4,
        out_specs=[vmem, vmem],
        out_shape=[
            jax.ShapeDtypeStruct((2, slots), f32),
            jax.ShapeDtypeStruct(prior.shape, f32),
        ],
        scratch_shapes=[
            pltpu.VMEM(by_slot.shape, bf16),
            pltpu.VMEM((rim, extent, slots), bf16),
            pltpu.VMEM((sum(down_sizes), extent, slots), bf16),
            pltpu.VMEM((sum(up_sizes), extent, slots), bf16),
            pltpu.VMEM((half + 2, padded, slots), f32),
            pltpu.VMEM((half + 4 + rim, padded, slots), f32),
            pltpu.VMEM((rim + 2, padded, slots), f32),
            pltpu.VMEM((padded, slots), f32),
            pltpu.VMEM((2, 9, 8, slots), f32),
            pltpu.SMEM((1, 1), jnp.int32),
            pltpu.VMEM((2, slots), jnp.int32),
            pltpu.VMEM((2, slots), jnp.int32),
            pltpu.VMEM(prior.shape, f32),
            pltpu.VMEM((2,) + prior.shape, f32),
            pltpu.VMEM((4, rows, 2 * cols), f32),
            pltpu.VMEM((2, rows, 2 * cols), f32),
            pltpu.VMEM((rows, 2 * cols), f32),
            pltpu.VMEM((8, slots), f32),
            pltpu.VMEM((8, slots), f32),
            pltpu.VMEM((16, slots), f32),
            pltpu.VMEM((16, slots), f32),
            pltpu.VMEM((16, slots), f32),
            pltpu.VMEM((16, slots), f32),
            pltpu.VMEM((16, slots), f32),
            sems((4,)),
            sems((len(up_sizes),)),
            sems((len(up_sizes),)),
            sems((len(down_sizes),)),
            sems((len(down_sizes),)),
            sems((2,)),
            sems((4,)),
            sems((2,)),
            sems((6,)),
        ],
        compiler_params=pltpu.CompilerParams(collective_id=0, has_side_effects=True),
    )(by_slot, counts, peak_shifts[0], prior)
    return flows[None], displacement[None, None]


def solution(mesh):
    placed = (
        P("sec", "tile", None, None),
        P("sec", "tile"),
        P("sec", None, "tile"),
        P("sec", "tile", None, None, None),
    )
    return jax.shard_map(
        body,
        mesh=mesh,
        in_specs=placed,
        out_specs=(P("sec", None, "tile"), P("sec", "tile", None, None, None)),
        check_vma=False,
    )
```

```python
import functools

import jax
import jax.numpy as jnp
from jax import lax
from jax.experimental import pallas as pl
from jax.experimental.pallas import tpu as pltpu
from jax.sharding import PartitionSpec as P

PCOLS = 16
ITERS = 8
REACH = 3
RIM = 8

MESH = pl.DeviceIdType.MESH


def chunk_sizes(extent):
    half, size = extent // 2, max(6, extent // 10)
    full = half // size - 1
    up = [size] * full + [half - size * full - 4, 4]
    down = [size] * full + [half - size * full - 4, 2 * REACH]
    return up, down


def build_shifted(dst, local, temp, base, low, high, row_shift, col_shift):
    extent = local.shape[0]
    row_shift = jnp.broadcast_to(row_shift, (extent, row_shift.shape[1]))
    col_shift = jnp.broadcast_to(col_shift, (extent, col_shift.shape[1]))

    def row(i, carry):
        total = None
        for k in range(-REACH, REACH + 1):
            at = base + i + k
            value = local[lax.rem(at + extent, extent)].astype(jnp.float32)
            if low > 0:
                value = value * jnp.where((at >= low) & (at < high), 1.0, 0.0)
            total = value if total is None else jnp.where(row_shift == k, value, total)
        temp[pl.ds(RIM, extent), :] = total
        temp[pl.ds(0, RIM), :] = total[extent - RIM :]
        temp[pl.ds(RIM + extent, RIM), :] = total[:RIM]
        total = None
        for k in range(-REACH, REACH + 1):
            value = temp[pl.ds(RIM + k, extent), :]
            total = value if total is None else jnp.where(col_shift == k, value, total)
        dst[i, pl.ds(RIM, extent), :] = total
        dst[i, pl.ds(0, RIM), :] = total[extent - RIM :]
        dst[i, pl.ds(RIM + extent, RIM), :] = total[:RIM]
        return carry

    lax.fori_loop(0, dst.shape[0], row, 0)


def add_lags(sums, other, start, shifted, first, count):
    extent, lanes = other.shape[1:]

    def row(i, totals):
        value = other[start + i].astype(jnp.float32)
        result = []
        for a in range(3):
            for b in range(3):
                product = value * shifted[first + i + a, pl.ds(RIM + b - 1, extent), :]
                total = totals[3 * a + b]
                for j in range(extent // 8):
                    total = total + product[8 * j : 8 * j + 8]
                result.append(total)
        return tuple(result)

    begun = tuple(sums[k] for k in range(9))
    for k, total in enumerate(lax.fori_loop(0, count, row, begun)):
        sums[k] = total


def slot_places(extent_lanes, lanes, cols, patch_cols, homes):
    slot = lax.broadcasted_iota(jnp.int32, (2 * lanes, extent_lanes), 0)
    lane = lax.broadcasted_iota(jnp.int32, (2 * lanes, extent_lanes), 1)
    within = slot % patch_cols
    column = jnp.where(slot < lanes, within, jnp.where(within == 0, patch_cols, -1))
    return jnp.where(column == homes(lane), 1.0, 0.0).astype(jnp.bfloat16)


def by_patch_row(line, patch_rows):
    shape = (patch_rows, line.shape[1])
    slots = patch_rows * PCOLS
    of = lax.broadcasted_iota(jnp.int32, shape, 1) % slots // PCOLS
    return jnp.where(of == lax.broadcasted_iota(jnp.int32, shape, 0), line, 0.0)


def flow_lines(scores, row_shift, col_shift, live):
    weights = [score * score for score in scores]
    total = 1.0 + sum(weights)
    row_part = (weights[6] + weights[7] + weights[8] - weights[0] - weights[1] - weights[2]) / total
    col_part = (weights[2] + weights[5] + weights[8] - weights[0] - weights[3] - weights[6]) / total
    return (
        jnp.where(live > 0.0, row_shift + row_part, 0.0),
        jnp.where(live > 0.0, col_shift + col_part, 0.0),
    )


def kernel(
    sections, tiles,
    patch_ref, count_ref, shift_ref, prior_ref,
    flow_ref, out_ref,
    local, merged, from_above, from_below, shifted_up, shifted_down, shifted_rim, temp, sums,
    count, shift, far_shift, prior, rims, far_rims, fields, goals, gain,
    info, east_info, part_up, part_down, own_up, east_up, east_down,
    local_sem, up_send, up_recv, down_send, down_recv,
    shift_sem, rim_sem, info_sem, part_sem,
):
    sec, tile = lax.axis_index("sec"), lax.axis_index("tile")
    extent, lanes = local.shape[1:]
    half = extent // 2
    rim = 2 * REACH
    low, high = half + REACH - 1, extent - REACH + 1
    up_sizes, down_sizes = chunk_sizes(extent)
    rows, cols = prior.shape[1:]
    patch_rows = lanes // PCOLS
    row_step, col_step = rows // patch_rows, cols // PCOLS
    has_below, has_above = sec > 0, sec < sections - 1
    has_west, has_east = tile > 0, tile < tiles - 1

    far_rims[...] = jnp.zeros_like(far_rims)
    for buffer in (info, east_info, part_up, part_down, own_up, east_up, east_down):
        buffer[...] = jnp.zeros_like(buffer)

    barrier = pltpu.get_barrier_semaphore()
    below, above = {"sec": sec - 1}, {"sec": sec + 1}
    west, east = {"tile": tile - 1}, {"tile": tile + 1}
    below_west = {"sec": sec - 1, "tile": tile - 1}
    partners = [
        (has_below, below),
        (has_above, above),
        (has_west, west),
        (has_east, east),
    ]

    def greet(where):
        return lambda: pl.semaphore_signal(
            barrier, 1, device_id=where, device_id_type=MESH
        )

    waits = 0
    for have, where in partners:
        pl.when(have)(greet(where))
        waits = waits + jnp.where(have, 1, 0)
    mine = [
        pltpu.make_async_copy(src, dst, local_sem.at[k])
        for k, (src, dst) in enumerate(
            ((shift_ref, shift), (count_ref, count), (prior_ref, prior), (patch_ref, local))
        )
    ]
    for copy in mine:
        copy.start()
    mine[0].wait()
    mine[1].wait()
    alive = jnp.where(
        lax.broadcasted_iota(jnp.int32, (1, lanes), 1) < count[0, 0], 1.0, 0.0
    )
    row_shift = shift[0:1, :].astype(jnp.float32)
    col_shift = shift[1:2, :].astype(jnp.float32)
    info[0:1, :] = row_shift
    info[1:2, :] = col_shift
    info[2:3, :] = alive
    mine[2].wait()
    for k in range(2):
        turned = jnp.transpose(prior[k])
        rims[0, k] = turned[:ITERS]
        rims[1, k] = turned[cols - ITERS :]
    pl.semaphore_wait(barrier, waits)

    def remote(src, dst, sems, k, where):
        return pltpu.make_async_remote_copy(
            src_ref=src,
            dst_ref=dst,
            send_sem=sems[0].at[k],
            recv_sem=sems[1].at[k],
            device_id=where,
            device_id_type=MESH,
        )

    def remote_at(src, dst, sems, k, where):
        send, recv = sems.at[2 * k], sems.at[2 * k + 1]
        return pltpu.make_async_remote_copy(
            src_ref=src, dst_ref=dst, send_sem=send, recv_sem=recv, device_id=where, device_id_type=MESH
        )

    shift_copy = remote_at(shift_ref, far_shift, shift_sem, 0, above)
    pl.when(has_above)(shift_copy.start)
    info_copy = remote_at(info, east_info, info_sem, 0, west)
    pl.when(has_west)(info_copy.start)
    to_east = remote_at(rims.at[1], far_rims.at[1], rim_sem, 0, east)
    to_west = remote_at(rims.at[0], far_rims.at[0], rim_sem, 1, west)
    pl.when(has_east)(to_east.start)
    pl.when(has_west)(to_west.start)
    ups, downs = [], []
    at = 0
    for c, size in enumerate(up_sizes):
        part = pl.ds(at, size)
        ups.append(remote(patch_ref.at[part], from_below.at[part], (up_send, up_recv), c, above))
        at += size
    at = 0
    for c, size in enumerate(down_sizes):
        part = pl.ds(at, size)
        source = merged if c == len(down_sizes) - 1 else patch_ref.at[pl.ds(low + at, size)]
        downs.append(remote(source, from_above.at[part], (down_send, down_recv), c, below))
        at += size
    for c in range(len(up_sizes)):
        pl.when(has_above)(ups[c].start)
        if c < len(down_sizes) - 1:
            pl.when(has_below)(downs[c].start)
    sums[...] = jnp.zeros_like(sums)
    mine[3].wait()

    @pl.when(has_below)
    def _():
        shift_copy.wait_recv()
        for j in range(rim):
            merged[j] = jnp.where(
                jnp.broadcast_to(far_shift[0:1, :], (extent, lanes)) <= j - REACH,
                local[half - REACH - 1 + j].astype(jnp.float32),
                local[(extent - REACH + 1 + j) % extent].astype(jnp.float32),
            ).astype(jnp.bfloat16)
        build_shifted(
            shifted_up, local, temp, -1, 0, extent, far_shift[0:1, :], far_shift[1:2, :]
        )
        downs[-1].start()

    @pl.when(has_above)
    def _():
        build_shifted(
            shifted_down, local, temp, half - REACH - 2, half, extent, -shift[0:1, :], -shift[1:2, :]
        )
        for i in range(rim + 2):
            shifted_rim[i] = shifted_down[i] + shifted_down[half + 2 + i]

    pl.when(has_west)(to_east.wait_recv)
    pl.when(has_east)(to_west.wait_recv)
    pl.when(has_east)(info_copy.wait_recv)
    lane = lax.broadcasted_iota(jnp.int32, (rows, cols), 1)
    in_east = (lane < ITERS) & has_east
    in_west = (lane >= cols - ITERS) & has_west
    for k in range(2):
        fields[k, :, :cols] = prior[k]
        between = jnp.zeros((cols - 2 * ITERS, rows), jnp.float32)
        fields[k, :, cols:] = jnp.transpose(
            jnp.concatenate([far_rims[0, k], between, far_rims[1, k]], 0)
        )
        fields[2 + k] = jnp.zeros((rows, 2 * cols), jnp.float32)
    inside = jnp.concatenate(
        [jnp.ones((rows, cols), jnp.float32), jnp.where(in_east | in_west, 1.0, 0.0)], 1
    )
    at_nodes = slot_places(
        2 * cols, lanes, cols, PCOLS,
        lambda lane: jnp.where(lane % col_step == 0, lane // col_step, -2),
    )
    both_alive = jnp.concatenate([alive, east_info[2:3, :]], 1)
    spots = jnp.dot(
        by_patch_row(both_alive, patch_rows).astype(jnp.bfloat16),
        at_nodes,
        preferred_element_type=jnp.float32,
    ).astype(jnp.bfloat16)
    spread = jnp.where(
        lax.broadcasted_iota(jnp.int32, (rows, patch_rows), 0)
        == row_step * lax.broadcasted_iota(jnp.int32, (rows, patch_rows), 1),
        1.0,
        0.0,
    ).astype(jnp.bfloat16)
    weight = jnp.dot(spread, spots, preferred_element_type=jnp.float32)
    gain[...] = (0.2 - 0.1 * weight) * inside
    wide_lane = lax.broadcasted_iota(jnp.int32, weight.shape, 1)
    for k in range(2):
        goals[k] = jnp.where(wide_lane // col_step % 2 == k, 0.4 * weight, 0.0)
    row = lax.broadcasted_iota(jnp.int32, weight.shape, 0)

    def sweep(_, carry):
        for k in range(4):
            field = fields[k]
            upper = jnp.where(row == 0, 0.0, pltpu.roll(field, 1, 0))
            lower = jnp.where(row == rows - 1, 0.0, pltpu.roll(field, rows - 1, 0))
            left = pltpu.roll(field, 1, 1)
            right = pltpu.roll(field, 2 * cols - 1, 1)
            field = 0.2 * field + gain[...] * ((upper + lower) + (left + right))
            fields[k] = field + goals[k - 2] if k >= 2 else field
        return carry

    lax.fori_loop(0, ITERS, sweep, 0)
    owners = slot_places(
        2 * cols, lanes, cols, PCOLS,
        lambda lane: jnp.where(
            lane < cols,
            2 * ((lane + col_step) // (2 * col_step)),
            2 * ((lane - cols) // (2 * col_step)) + 1,
        ),
    )

    up_at = down_at = 0
    for c, (up_size, down_size) in enumerate(zip(up_sizes, down_sizes, strict=True)):
        final = c == len(up_sizes) - 1

        @pl.when(has_below)
        def _():
            ups[c].wait_recv()
            add_lags(sums.at[0], from_below, up_at, shifted_up, up_at, up_size)

        if final:

            @pl.when(has_below)
            def _():
                for k in range(9):
                    part_up[k : k + 1, :] = jnp.sum(sums[0, k], axis=0, keepdims=True)

            up_part = remote_at(part_up, own_up, part_sem, 0, below)
            up_part_west = remote_at(part_up, east_up, part_sem, 1, below_west)
            pl.when(has_below)(up_part.start)
            pl.when(has_below & has_west)(up_part_west.start)

        @pl.when(has_above)
        def _():
            downs[c].wait_recv()
            if final:
                add_lags(sums.at[1], from_above, down_at, shifted_rim, 0, down_size)
            else:
                add_lags(sums.at[1], from_above, down_at, shifted_down, down_at + rim, down_size)

        up_at += up_size
        down_at += down_size

    for k in range(9):
        part_down[k : k + 1, :] = jnp.sum(sums[1, 8 - k], axis=0, keepdims=True)
    down_part = remote_at(part_down, east_down, part_sem, 2, west)
    pl.when(has_west)(down_part.start)

    pl.when(has_above)(up_part.wait_recv)
    scale = float(extent)
    flow_a, flow_b = flow_lines(
        [(part_down[k : k + 1, :] + own_up[k : k + 1, :]) / scale for k in range(9)],
        row_shift,
        col_shift,
        alive,
    )
    flow_ref[0:1, :] = flow_a
    flow_ref[1:2, :] = flow_b
    pl.when(has_east)(down_part.wait_recv)
    pl.when(has_above & has_east)(up_part_west.wait_recv)
    east_a, east_b = flow_lines(
        [(east_down[k : k + 1, :] + east_up[k : k + 1, :]) / scale for k in range(9)],
        east_info[0:1, :],
        east_info[1:2, :],
        east_info[2:3, :],
    )
    left = jnp.concatenate(
        [
            by_patch_row(jnp.concatenate([flow_a, east_a], 1), patch_rows),
            by_patch_row(jnp.concatenate([flow_b, east_b], 1), patch_rows),
        ],
        0,
    )
    first = left.astype(jnp.bfloat16)
    rest = left - first.astype(jnp.float32)
    second = rest.astype(jnp.bfloat16)
    third = (rest - second.astype(jnp.float32)).astype(jnp.bfloat16)
    values = sum(
        jnp.dot(piece, owners, preferred_element_type=jnp.float32)
        for piece in (first, second, third)
    )
    strip = row_step // 2
    for m in range(rows // strip):
        owner = (m + 1) // 2
        part = pl.ds(m * strip, strip)
        for k in range(2):
            result = fields[k, part, :cols]
            if owner < patch_rows:
                value = values[k * patch_rows + owner : k * patch_rows + owner + 1]
                result = (
                    result
                    + fields[2, part, :cols] * value[:, :cols]
                    + fields[3, part, :cols] * value[:, cols:]
                )
            out_ref[k, part, :] = result

    pl.when(has_above)(shift_copy.wait_send)
    for copy in ups:
        pl.when(has_above)(copy.wait_send)
    for copy in downs:
        pl.when(has_below)(copy.wait_send)
    pl.when(has_east)(to_east.wait_send)
    pl.when(has_west)(to_west.wait_send)
    pl.when(has_west)(info_copy.wait_send)
    pl.when(has_below)(up_part.wait_send)
    pl.when(has_below & has_west)(up_part_west.wait_send)
    pl.when(has_west)(down_part.wait_send)


def body(patches, counts, peak_shifts, mesh_prior):
    sections, tiles = lax.axis_size("sec"), lax.axis_size("tile")
    by_slot = jnp.transpose(patches[0], (1, 2, 0))
    extent, _, slots = by_slot.shape
    prior = mesh_prior[0, 0]
    rows, cols = prior.shape[1:]
    half, rim = extent // 2, 2 * REACH
    up_sizes, down_sizes = chunk_sizes(extent)
    padded = extent + 2 * RIM
    sems = pltpu.SemaphoreType.DMA
    vmem = pl.BlockSpec(memory_space=pltpu.VMEM)
    f32, bf16 = jnp.float32, jnp.bfloat16
    flows, displacement = pl.pallas_call(
        functools.partial(kernel, sections, tiles),
        in_specs=[pl.BlockSpec(memory_space=pltpu.HBM)] * 4,
        out_specs=[vmem, vmem],
        out_shape=[
            jax.ShapeDtypeStruct((2, slots), f32),
            jax.ShapeDtypeStruct(prior.shape, f32),
        ],
        scratch_shapes=[
            pltpu.VMEM(by_slot.shape, bf16),
            pltpu.VMEM((rim, extent, slots), bf16),
            pltpu.VMEM((sum(down_sizes), extent, slots), bf16),
            pltpu.VMEM((sum(up_sizes), extent, slots), bf16),
            pltpu.VMEM((half + 2, padded, slots), f32),
            pltpu.VMEM((half + 4 + rim, padded, slots), f32),
            pltpu.VMEM((rim + 2, padded, slots), f32),
            pltpu.VMEM((padded, slots), f32),
            pltpu.VMEM((2, 9, 8, slots), f32),
            pltpu.SMEM((1, 1), jnp.int32),
            pltpu.VMEM((2, slots), jnp.int32),
            pltpu.VMEM((2, slots), jnp.int32),
            pltpu.VMEM(prior.shape, f32),
            pltpu.VMEM((2, 2, ITERS, rows), f32),
            pltpu.VMEM((2, 2, ITERS, rows), f32),
            pltpu.VMEM((4, rows, 2 * cols), f32),
            pltpu.VMEM((2, rows, 2 * cols), f32),
            pltpu.VMEM((rows, 2 * cols), f32),
            pltpu.VMEM((8, slots), f32),
            pltpu.VMEM((8, slots), f32),
            pltpu.VMEM((16, slots), f32),
            pltpu.VMEM((16, slots), f32),
            pltpu.VMEM((16, slots), f32),
            pltpu.VMEM((16, slots), f32),
            pltpu.VMEM((16, slots), f32),
            sems((4,)),
            sems((len(up_sizes),)),
            sems((len(up_sizes),)),
            sems((len(down_sizes),)),
            sems((len(down_sizes),)),
            sems((2,)),
            sems((4,)),
            sems((2,)),
            sems((6,)),
        ],
        compiler_params=pltpu.CompilerParams(collective_id=0, has_side_effects=True),
    )(by_slot, counts, peak_shifts[0], prior)
    return flows[None], displacement[None, None]


def solution(mesh):
    placed = (
        P("sec", "tile", None, None),
        P("sec", "tile"),
        P("sec", None, "tile"),
        P("sec", "tile", None, None, None),
    )
    return jax.shard_map(
        body,
        mesh=mesh,
        in_specs=placed,
        out_specs=(P("sec", None, "tile"), P("sec", "tile", None, None, None)),
        check_vma=False,
    )
```

```python
import functools

import jax
import jax.numpy as jnp
from jax import lax
from jax.experimental import pallas as pl
from jax.experimental.pallas import tpu as pltpu
from jax.sharding import PartitionSpec as P

PCOLS = 16
ITERS = 8
REACH = 3
RIM = 8

MESH = pl.DeviceIdType.MESH


def rows_up(extent):
    return extent // 2 - 1


def chunk_sizes(extent):
    size = max(6, extent // 10)
    full = extent // 2 // size - 1
    sent = rows_up(extent)
    up = [size] * full + [sent - size * full - 4, 4]
    down = [size] * full + [extent - sent - REACH - 1 - size * full, 2 * REACH]
    return up, down


def build_shifted(dst, local, temp, base, low, high, row_shift, col_shift):
    extent = local.shape[0]
    row_shift = jnp.broadcast_to(row_shift, (extent, row_shift.shape[1]))
    col_shift = jnp.broadcast_to(col_shift, (extent, col_shift.shape[1]))

    def row(i, carry):
        total = None
        for k in range(-REACH, REACH + 1):
            at = base + i + k
            value = local[lax.rem(at + extent, extent)].astype(jnp.float32)
            if low > 0:
                value = value * jnp.where((at >= low) & (at < high), 1.0, 0.0)
            total = value if total is None else jnp.where(row_shift == k, value, total)
        temp[pl.ds(RIM, extent), :] = total
        temp[pl.ds(0, RIM), :] = total[extent - RIM :]
        temp[pl.ds(RIM + extent, RIM), :] = total[:RIM]
        total = None
        for k in range(-REACH, REACH + 1):
            value = temp[pl.ds(RIM + k, extent), :]
            total = value if total is None else jnp.where(col_shift == k, value, total)
        dst[i, pl.ds(RIM, extent), :] = total
        dst[i, pl.ds(0, RIM), :] = total[extent - RIM :]
        dst[i, pl.ds(RIM + extent, RIM), :] = total[:RIM]
        return carry

    lax.fori_loop(0, dst.shape[0], row, 0)


def add_lags(sums, other, start, shifted, first, count):
    extent, lanes = other.shape[1:]

    def row(i, totals):
        value = other[start + i].astype(jnp.float32)
        result = []
        for a in range(3):
            for b in range(3):
                product = value * shifted[first + i + a, pl.ds(RIM + b - 1, extent), :]
                total = totals[3 * a + b]
                for j in range(extent // 8):
                    total = total + product[8 * j : 8 * j + 8]
                result.append(total)
        return tuple(result)

    begun = tuple(sums[k] for k in range(9))
    for k, total in enumerate(lax.fori_loop(0, count, row, begun)):
        sums[k] = total


def slot_places(extent_lanes, lanes, cols, patch_cols, homes):
    slot = lax.broadcasted_iota(jnp.int32, (2 * lanes, extent_lanes), 0)
    lane = lax.broadcasted_iota(jnp.int32, (2 * lanes, extent_lanes), 1)
    within = slot % patch_cols
    column = jnp.where(slot < lanes, within, jnp.where(within == 0, patch_cols, -1))
    return jnp.where(column == homes(lane), 1.0, 0.0).astype(jnp.bfloat16)


def by_patch_row(line, patch_rows):
    shape = (patch_rows, line.shape[1])
    slots = patch_rows * PCOLS
    of = lax.broadcasted_iota(jnp.int32, shape, 1) % slots // PCOLS
    return jnp.where(of == lax.broadcasted_iota(jnp.int32, shape, 0), line, 0.0)


def flow_lines(scores, row_shift, col_shift, live):
    weights = [score * score for score in scores]
    total = 1.0 + sum(weights)
    row_part = (weights[6] + weights[7] + weights[8] - weights[0] - weights[1] - weights[2]) / total
    col_part = (weights[2] + weights[5] + weights[8] - weights[0] - weights[3] - weights[6]) / total
    return (
        jnp.where(live > 0.0, row_shift + row_part, 0.0),
        jnp.where(live > 0.0, col_shift + col_part, 0.0),
    )


def kernel(
    sections, tiles,
    patch_ref, count_ref, shift_ref, prior_ref,
    line_ref, base_ref, owner_ref,
    local, merged, from_above, from_below, shifted_up, shifted_down, shifted_rim, temp, sums,
    count, shift, far_shift, prior, rims, far_rims, fields, goals, gain,
    info, east_info, part_up, part_down, own_up, east_up, east_down,
    local_sem, up_send, up_recv, down_send, down_recv,
    shift_sem, rim_sem, info_sem, part_sem,
):
    sec, tile = lax.axis_index("sec"), lax.axis_index("tile")
    extent, lanes = local.shape[1:]
    sent = rows_up(extent)
    rim = 2 * REACH
    low = sent + REACH - 1
    up_sizes, down_sizes = chunk_sizes(extent)
    rows, cols = prior.shape[1:]
    patch_rows = lanes // PCOLS
    row_step, col_step = rows // patch_rows, cols // PCOLS
    has_below, has_above = sec > 0, sec < sections - 1
    has_west, has_east = tile > 0, tile < tiles - 1
    even = lax.rem(tile, 2) == 0

    far_rims[...] = jnp.zeros_like(far_rims)
    line_ref[...] = jnp.zeros_like(line_ref)
    for buffer in (info, east_info, part_up, part_down, own_up, east_up, east_down):
        buffer[...] = jnp.zeros_like(buffer)

    barrier = pltpu.get_barrier_semaphore()
    below, above = {"sec": sec - 1}, {"sec": sec + 1}
    west, east = {"tile": tile - 1}, {"tile": tile + 1}
    below_west = {"sec": sec - 1, "tile": tile - 1}
    partners = [
        (has_below, below),
        (has_above, above),
        (has_west, west),
        (has_east, east),
    ]

    def greet(where):
        return lambda: pl.semaphore_signal(
            barrier, 1, device_id=where, device_id_type=MESH
        )

    waits = 0
    for have, where in partners:
        pl.when(have)(greet(where))
        waits = waits + jnp.where(have, 1, 0)
    mine = [
        pltpu.make_async_copy(src, dst, local_sem.at[k])
        for k, (src, dst) in enumerate(
            ((shift_ref, shift), (count_ref, count), (prior_ref, prior), (patch_ref, local))
        )
    ]
    for copy in mine:
        copy.start()
    mine[0].wait()
    mine[1].wait()
    alive = jnp.where(
        lax.broadcasted_iota(jnp.int32, (1, lanes), 1) < count[0, 0], 1.0, 0.0
    )
    row_shift = shift[0:1, :].astype(jnp.float32)
    col_shift = shift[1:2, :].astype(jnp.float32)
    info[0:1, :] = row_shift
    info[1:2, :] = col_shift
    info[2:3, :] = alive
    mine[2].wait()
    for k in range(2):
        turned = jnp.transpose(prior[k])
        rims[0, k] = turned[:ITERS]
        rims[1, k] = turned[cols - ITERS :]
    pl.semaphore_wait(barrier, waits)

    def remote(src, dst, sems, k, where):
        return pltpu.make_async_remote_copy(
            src_ref=src,
            dst_ref=dst,
            send_sem=sems[0].at[k],
            recv_sem=sems[1].at[k],
            device_id=where,
            device_id_type=MESH,
        )

    def remote_at(src, dst, sems, k, where):
        send, recv = sems.at[2 * k], sems.at[2 * k + 1]
        return pltpu.make_async_remote_copy(
            src_ref=src, dst_ref=dst, send_sem=send, recv_sem=recv, device_id=where, device_id_type=MESH
        )

    shift_copy = remote_at(shift_ref, far_shift, shift_sem, 0, above)
    pl.when(has_above)(shift_copy.start)
    info_copy = remote_at(info, east_info, info_sem, 0, west)
    pl.when(has_west)(info_copy.start)
    to_east = remote_at(rims.at[1], far_rims.at[1], rim_sem, 0, east)
    to_west = remote_at(rims.at[0], far_rims.at[0], rim_sem, 1, west)
    pl.when(has_east)(to_east.start)
    pl.when(has_west)(to_west.start)
    ups, downs = [], []
    at = 0
    for c, size in enumerate(up_sizes):
        part = pl.ds(at, size)
        ups.append(remote(patch_ref.at[part], from_below.at[part], (up_send, up_recv), c, above))
        at += size
    at = 0
    for c, size in enumerate(down_sizes):
        part = pl.ds(at, size)
        source = merged if c == len(down_sizes) - 1 else patch_ref.at[pl.ds(low + at, size)]
        downs.append(remote(source, from_above.at[part], (down_send, down_recv), c, below))
        at += size
    for c in range(len(up_sizes)):
        pl.when(has_above)(ups[c].start)
        if c < len(down_sizes) - 1:
            pl.when(has_below)(downs[c].start)
    sums[...] = jnp.zeros_like(sums)
    mine[3].wait()

    @pl.when(has_below)
    def _():
        shift_copy.wait_recv()
        for j in range(rim):
            merged[j] = jnp.where(
                jnp.broadcast_to(far_shift[0:1, :], (extent, lanes)) <= j - REACH,
                local[sent - REACH - 1 + j].astype(jnp.float32),
                local[(extent - REACH + 1 + j) % extent].astype(jnp.float32),
            ).astype(jnp.bfloat16)
        build_shifted(
            shifted_up, local, temp, -1, 0, extent, far_shift[0:1, :], far_shift[1:2, :]
        )
        pl.when(even)(downs[-1].start)

    @pl.when(has_above)
    def _():
        build_shifted(
            shifted_down, local, temp, sent - REACH - 2, sent, extent, -shift[0:1, :], -shift[1:2, :]
        )
        for i in range(rim + 2):
            shifted_rim[i] = shifted_down[i] + shifted_down[extent - sent + 2 + i]

    pl.when(has_west)(to_east.wait_recv)
    pl.when(has_east)(to_west.wait_recv)
    pl.when(has_east)(info_copy.wait_recv)
    lane = lax.broadcasted_iota(jnp.int32, (rows, cols), 1)
    in_east = (lane < ITERS) & has_east
    in_west = (lane >= cols - ITERS) & has_west
    for k in range(2):
        fields[k, :, :cols] = prior[k]
        between = jnp.zeros((cols - 2 * ITERS, rows), jnp.float32)
        fields[k, :, cols:] = jnp.transpose(
            jnp.concatenate([far_rims[0, k], between, far_rims[1, k]], 0)
        )
        fields[2 + k] = jnp.zeros((rows, 2 * cols), jnp.float32)
    inside = jnp.concatenate(
        [jnp.ones((rows, cols), jnp.float32), jnp.where(in_east | in_west, 1.0, 0.0)], 1
    )
    at_nodes = slot_places(
        2 * cols, lanes, cols, PCOLS,
        lambda lane: jnp.where(lane % col_step == 0, lane // col_step, -2),
    )
    both_alive = jnp.concatenate([alive, east_info[2:3, :]], 1)
    spots = jnp.dot(
        by_patch_row(both_alive, patch_rows).astype(jnp.bfloat16),
        at_nodes,
        preferred_element_type=jnp.float32,
    ).astype(jnp.bfloat16)
    spread = jnp.where(
        lax.broadcasted_iota(jnp.int32, (rows, patch_rows), 0)
        == row_step * lax.broadcasted_iota(jnp.int32, (rows, patch_rows), 1),
        1.0,
        0.0,
    ).astype(jnp.bfloat16)
    weight = jnp.dot(spread, spots, preferred_element_type=jnp.float32)
    gain[...] = (0.2 - 0.1 * weight) * inside
    wide_lane = lax.broadcasted_iota(jnp.int32, weight.shape, 1)
    for k in range(2):
        goals[k] = jnp.where(wide_lane // col_step % 2 == k, 0.4 * weight, 0.0)
    row = lax.broadcasted_iota(jnp.int32, weight.shape, 0)

    def sweep(_, carry):
        for k in range(4):
            field = fields[k]
            upper = jnp.where(row == 0, 0.0, pltpu.roll(field, 1, 0))
            lower = jnp.where(row == rows - 1, 0.0, pltpu.roll(field, rows - 1, 0))
            left = pltpu.roll(field, 1, 1)
            right = pltpu.roll(field, 2 * cols - 1, 1)
            field = 0.2 * field + gain[...] * ((upper + lower) + (left + right))
            fields[k] = field + goals[k - 2] if k >= 2 else field
        return carry

    lax.fori_loop(0, ITERS, sweep, 0)
    for k in range(4):
        base_ref[k] = fields[k, :, :cols]
    owner_ref[...] = slot_places(
        2 * cols, lanes, cols, PCOLS,
        lambda lane: jnp.where(
            lane < cols,
            2 * ((lane + col_step) // (2 * col_step)),
            2 * ((lane - cols) // (2 * col_step)) + 1,
        ),
    )

    up_at = down_at = 0
    for c, (up_size, down_size) in enumerate(zip(up_sizes, down_sizes, strict=True)):
        final = c == len(up_sizes) - 1

        @pl.when(has_below)
        def _():
            ups[c].wait_recv()
            add_lags(sums.at[0], from_below, up_at, shifted_up, up_at, up_size)

        if final:

            @pl.when(has_below)
            def _():
                for k in range(9):
                    part_up[k : k + 1, :] = jnp.sum(sums[0, k], axis=0, keepdims=True)

            up_part = remote_at(part_up, own_up, part_sem, 0, below)
            up_part_west = remote_at(part_up, east_up, part_sem, 1, below_west)
            pl.when(has_below)(up_part.start)
            pl.when(has_below & has_west)(up_part_west.start)

        @pl.when(has_above)
        def _():
            downs[c].wait_recv()
            if final:
                add_lags(sums.at[1], from_above, down_at, shifted_rim, 0, down_size)
            else:
                add_lags(sums.at[1], from_above, down_at, shifted_down, down_at + rim, down_size)

        if c == len(up_sizes) - 2:
            pl.when(has_below & ~even)(downs[-1].start)
        up_at += up_size
        down_at += down_size

    for k in range(9):
        part_down[k : k + 1, :] = jnp.sum(sums[1, 8 - k], axis=0, keepdims=True)
    down_part = remote_at(part_down, east_down, part_sem, 2, west)
    pl.when(has_west)(down_part.start)

    pl.when(has_above)(up_part.wait_recv)
    scale = float(extent)
    flow_a, flow_b = flow_lines(
        [(part_down[k : k + 1, :] + own_up[k : k + 1, :]) / scale for k in range(9)],
        row_shift,
        col_shift,
        alive,
    )
    line_ref[0:1, :] = flow_a
    line_ref[1:2, :] = flow_b
    pl.when(has_east)(down_part.wait_recv)
    pl.when(has_above & has_east)(up_part_west.wait_recv)
    east_a, east_b = flow_lines(
        [(east_down[k : k + 1, :] + east_up[k : k + 1, :]) / scale for k in range(9)],
        east_info[0:1, :],
        east_info[1:2, :],
        east_info[2:3, :],
    )
    line_ref[2:3, :] = east_a
    line_ref[3:4, :] = east_b

    pl.when(has_above)(shift_copy.wait_send)
    for copy in ups:
        pl.when(has_above)(copy.wait_send)
    for copy in downs:
        pl.when(has_below)(copy.wait_send)
    pl.when(has_east)(to_east.wait_send)
    pl.when(has_west)(to_west.wait_send)
    pl.when(has_west)(info_copy.wait_send)
    pl.when(has_below)(up_part.wait_send)
    pl.when(has_below & has_west)(up_part_west.wait_send)
    pl.when(has_west)(down_part.wait_send)


def finish_kernel(line_ref, base_ref, owner_ref, flow_ref, out_ref):
    rows, cols = base_ref.shape[1:]
    patch_rows = line_ref.shape[1] // PCOLS
    step = rows // patch_rows
    flow_ref[...] = line_ref[0:2, :]
    left = jnp.concatenate(
        [
            by_patch_row(
                jnp.concatenate([line_ref[k : k + 1, :], line_ref[k + 2 : k + 3, :]], 1), patch_rows
            )
            for k in range(2)
        ],
        0,
    )
    first = left.astype(jnp.bfloat16)
    rest = left - first.astype(jnp.float32)
    second = rest.astype(jnp.bfloat16)
    third = (rest - second.astype(jnp.float32)).astype(jnp.bfloat16)
    parts = jnp.dot(
        jnp.concatenate([first, second, third], 0), owner_ref[...], preferred_element_type=jnp.float32
    )
    size = 2 * patch_rows
    values = parts[:size] + parts[size : 2 * size] + parts[2 * size :]
    strip = step // 2
    for m in range(rows // strip):
        owner = (m + 1) // 2
        part = pl.ds(m * strip, strip)
        for k in range(2):
            result = base_ref[k, part, :]
            if owner < patch_rows:
                value = values[k * patch_rows + owner : k * patch_rows + owner + 1]
                result = (
                    result
                    + base_ref[2, part, :] * value[:, :cols]
                    + base_ref[3, part, :] * value[:, cols:]
                )
            out_ref[k, part, :] = result


def body(patches, counts, peak_shifts, mesh_prior):
    sections, tiles = lax.axis_size("sec"), lax.axis_size("tile")
    by_slot = jnp.transpose(patches[0], (1, 2, 0))
    extent, _, slots = by_slot.shape
    prior = mesh_prior[0, 0]
    rows, cols = prior.shape[1:]
    sent, rim = rows_up(extent), 2 * REACH
    up_sizes, down_sizes = chunk_sizes(extent)
    padded = extent + 2 * RIM
    sems = pltpu.SemaphoreType.DMA
    vmem = pl.BlockSpec(memory_space=pltpu.VMEM)
    f32, bf16 = jnp.float32, jnp.bfloat16
    lines, base, owners = pl.pallas_call(
        functools.partial(kernel, sections, tiles),
        in_specs=[pl.BlockSpec(memory_space=pltpu.HBM)] * 4,
        out_specs=[vmem, vmem, vmem],
        out_shape=[
            pltpu.VMEM((8, slots), f32),
            pltpu.VMEM((4, rows, cols), f32),
            pltpu.VMEM((2 * slots, 2 * cols), bf16),
        ],
        scratch_shapes=[
            pltpu.VMEM(by_slot.shape, bf16),
            pltpu.VMEM((rim, extent, slots), bf16),
            pltpu.VMEM((sum(down_sizes), extent, slots), bf16),
            pltpu.VMEM((sum(up_sizes), extent, slots), bf16),
            pltpu.VMEM((sent + 2, padded, slots), f32),
            pltpu.VMEM((extent - sent + 4 + rim, padded, slots), f32),
            pltpu.VMEM((rim + 2, padded, slots), f32),
            pltpu.VMEM((padded, slots), f32),
            pltpu.VMEM((2, 9, 8, slots), f32),
            pltpu.SMEM((1, 1), jnp.int32),
            pltpu.VMEM((2, slots), jnp.int32),
            pltpu.VMEM((2, slots), jnp.int32),
            pltpu.VMEM(prior.shape, f32),
            pltpu.VMEM((2, 2, ITERS, rows), f32),
            pltpu.VMEM((2, 2, ITERS, rows), f32),
            pltpu.VMEM((4, rows, 2 * cols), f32),
            pltpu.VMEM((2, rows, 2 * cols), f32),
            pltpu.VMEM((rows, 2 * cols), f32),
            pltpu.VMEM((8, slots), f32),
            pltpu.VMEM((8, slots), f32),
            pltpu.VMEM((16, slots), f32),
            pltpu.VMEM((16, slots), f32),
            pltpu.VMEM((16, slots), f32),
            pltpu.VMEM((16, slots), f32),
            pltpu.VMEM((16, slots), f32),
            sems((4,)),
            sems((len(up_sizes),)),
            sems((len(up_sizes),)),
            sems((len(down_sizes),)),
            sems((len(down_sizes),)),
            sems((2,)),
            sems((4,)),
            sems((2,)),
            sems((6,)),
        ],
        compiler_params=pltpu.CompilerParams(collective_id=0, has_side_effects=True),
    )(by_slot, counts, peak_shifts[0], prior)
    flows, displacement = pl.pallas_call(
        finish_kernel,
        in_specs=[vmem, vmem, vmem],
        out_specs=[vmem, vmem],
        out_shape=[
            jax.ShapeDtypeStruct((2, slots), f32),
            jax.ShapeDtypeStruct(prior.shape, f32),
        ],
    )(*[pltpu.with_memory_space_constraint(x, pltpu.VMEM) for x in (lines, base, owners)])
    return flows[None], displacement[None, None]


def solution(mesh):
    placed = (
        P("sec", "tile", None, None),
        P("sec", "tile"),
        P("sec", None, "tile"),
        P("sec", "tile", None, None, None),
    )
    return jax.shard_map(
        body,
        mesh=mesh,
        in_specs=placed,
        out_specs=(P("sec", None, "tile"), P("sec", "tile", None, None, None)),
        check_vma=False,
    )
```

```python
import functools

import jax
import jax.numpy as jnp
from jax import lax
from jax.experimental import pallas as pl
from jax.experimental.pallas import tpu as pltpu
from jax.sharding import PartitionSpec as P

PCOLS = 16
ITERS = 8
REACH = 3
RIM = 8

MESH = pl.DeviceIdType.MESH


def rows_up(extent):
    return extent // 2 + 1


def chunk_sizes(extent):
    size = max(6, extent // 10)
    full = extent // 2 // size - 1
    sent = rows_up(extent)
    up = [size] * full + [sent - size * full - 4, 4]
    down = [size] * full + [extent - sent - REACH - 1 - size * full, 2 * REACH]
    return up, down


def build_shifted(dst, local, temp, base, low, high, row_shift, col_shift):
    extent = local.shape[0]
    row_shift = jnp.broadcast_to(row_shift, (extent, row_shift.shape[1]))
    col_shift = jnp.broadcast_to(col_shift, (extent, col_shift.shape[1]))

    def row(i, carry):
        total = None
        for k in range(-REACH, REACH + 1):
            at = base + i + k
            value = local[lax.rem(at + extent, extent)].astype(jnp.float32)
            if low > 0:
                value = value * jnp.where((at >= low) & (at < high), 1.0, 0.0)
            total = value if total is None else jnp.where(row_shift == k, value, total)
        temp[pl.ds(RIM, extent), :] = total
        temp[pl.ds(0, RIM), :] = total[extent - RIM :]
        temp[pl.ds(RIM + extent, RIM), :] = total[:RIM]
        total = None
        for k in range(-REACH, REACH + 1):
            value = temp[pl.ds(RIM + k, extent), :]
            total = value if total is None else jnp.where(col_shift == k, value, total)
        dst[i, pl.ds(RIM, extent), :] = total
        dst[i, pl.ds(0, RIM), :] = total[extent - RIM :]
        dst[i, pl.ds(RIM + extent, RIM), :] = total[:RIM]
        return carry

    lax.fori_loop(0, dst.shape[0], row, 0)


def add_lags(sums, other, start, shifted, first, count):
    extent, lanes = other.shape[1:]

    def row(i, totals):
        value = other[start + i].astype(jnp.float32)
        result = []
        for a in range(3):
            for b in range(3):
                product = value * shifted[first + i + a, pl.ds(RIM + b - 1, extent), :]
                total = totals[3 * a + b]
                for j in range(extent // 8):
                    total = total + product[8 * j : 8 * j + 8]
                result.append(total)
        return tuple(result)

    begun = tuple(sums[k] for k in range(9))
    for k, total in enumerate(lax.fori_loop(0, count, row, begun)):
        sums[k] = total


def slot_places(extent_lanes, lanes, cols, patch_cols, homes):
    slot = lax.broadcasted_iota(jnp.int32, (2 * lanes, extent_lanes), 0)
    lane = lax.broadcasted_iota(jnp.int32, (2 * lanes, extent_lanes), 1)
    within = slot % patch_cols
    column = jnp.where(slot < lanes, within, jnp.where(within == 0, patch_cols, -1))
    return jnp.where(column == homes(lane), 1.0, 0.0).astype(jnp.bfloat16)


def by_patch_row(line, patch_rows):
    shape = (patch_rows, line.shape[1])
    slots = patch_rows * PCOLS
    of = lax.broadcasted_iota(jnp.int32, shape, 1) % slots // PCOLS
    return jnp.where(of == lax.broadcasted_iota(jnp.int32, shape, 0), line, 0.0)


def flow_lines(scores, row_shift, col_shift, live):
    weights = [score * score for score in scores]
    total = 1.0 + sum(weights)
    row_part = (weights[6] + weights[7] + weights[8] - weights[0] - weights[1] - weights[2]) / total
    col_part = (weights[2] + weights[5] + weights[8] - weights[0] - weights[3] - weights[6]) / total
    return (
        jnp.where(live > 0.0, row_shift + row_part, 0.0),
        jnp.where(live > 0.0, col_shift + col_part, 0.0),
    )


def kernel(
    sections, tiles,
    patch_ref, count_ref, shift_ref, prior_ref,
    line_ref, base_ref, owner_ref,
    local, merged, from_above, from_below, shifted_up, shifted_down, shifted_rim, temp, sums,
    count, shift, far_shift, prior, rims, far_rims, fields, goals, gain,
    info, east_info, part_up, part_down, own_up, east_up, east_down,
    local_sem, up_send, up_recv, down_send, down_recv,
    shift_sem, rim_sem, info_sem, part_sem, relay_sem,
):
    sec, tile = lax.axis_index("sec"), lax.axis_index("tile")
    extent, lanes = local.shape[1:]
    sent = rows_up(extent)
    rim = 2 * REACH
    low = sent + REACH - 1
    up_sizes, down_sizes = chunk_sizes(extent)
    rows, cols = prior.shape[1:]
    patch_rows = lanes // PCOLS
    row_step, col_step = rows // patch_rows, cols // PCOLS
    has_below, has_above = sec > 0, sec < sections - 1
    has_west, has_east = tile > 0, tile < tiles - 1
    even = lax.rem(tile, 2) == 0
    middle, relay = sections // 2, len(up_sizes) - 2
    is_low, is_high = sec == middle - 1, sec == middle
    is_first, is_last = sec == 0, sec == sections - 1
    late_up, late_down = ~even & ~is_low, ~even & ~is_high

    far_rims[...] = jnp.zeros_like(far_rims)
    line_ref[...] = jnp.zeros_like(line_ref)
    for buffer in (info, east_info, part_up, part_down, own_up, east_up, east_down):
        buffer[...] = jnp.zeros_like(buffer)

    barrier = pltpu.get_barrier_semaphore()
    below, above = {"sec": sec - 1}, {"sec": sec + 1}
    west, east = {"tile": tile - 1}, {"tile": tile + 1}
    below_west = {"sec": sec - 1, "tile": tile - 1}
    partners = [
        (has_below, below),
        (has_above, above),
        (has_west, west),
        (has_east, east),
        (is_first, {"sec": middle}),
        (is_last, {"sec": middle - 1}),
    ]
    greeted = [has_below, has_above, has_west, has_east, is_low, is_high]

    def greet(where):
        return lambda: pl.semaphore_signal(
            barrier, 1, device_id=where, device_id_type=MESH
        )

    for have, where in partners:
        pl.when(have)(greet(where))
    waits = sum(jnp.where(have, 1, 0) for have in greeted)
    mine = [
        pltpu.make_async_copy(src, dst, local_sem.at[k])
        for k, (src, dst) in enumerate(
            ((shift_ref, shift), (count_ref, count), (prior_ref, prior), (patch_ref, local))
        )
    ]
    for copy in mine:
        copy.start()
    mine[0].wait()
    mine[1].wait()
    alive = jnp.where(
        lax.broadcasted_iota(jnp.int32, (1, lanes), 1) < count[0, 0], 1.0, 0.0
    )
    row_shift = shift[0:1, :].astype(jnp.float32)
    col_shift = shift[1:2, :].astype(jnp.float32)
    info[0:1, :] = row_shift
    info[1:2, :] = col_shift
    info[2:3, :] = alive
    mine[2].wait()
    for k in range(2):
        turned = jnp.transpose(prior[k])
        rims[0, k] = turned[:ITERS]
        rims[1, k] = turned[cols - ITERS :]
    pl.semaphore_wait(barrier, waits)

    def remote(src, dst, sems, k, where):
        return pltpu.make_async_remote_copy(
            src_ref=src,
            dst_ref=dst,
            send_sem=sems[0].at[k],
            recv_sem=sems[1].at[k],
            device_id=where,
            device_id_type=MESH,
        )

    def remote_at(src, dst, sems, k, where):
        send, recv = sems.at[2 * k], sems.at[2 * k + 1]
        return pltpu.make_async_remote_copy(
            src_ref=src, dst_ref=dst, send_sem=send, recv_sem=recv, device_id=where, device_id_type=MESH
        )

    shift_copy = remote_at(shift_ref, far_shift, shift_sem, 0, above)
    pl.when(has_above)(shift_copy.start)
    info_copy = remote_at(info, east_info, info_sem, 0, west)
    pl.when(has_west)(info_copy.start)
    to_east = remote_at(rims.at[1], far_rims.at[1], rim_sem, 0, east)
    to_west = remote_at(rims.at[0], far_rims.at[0], rim_sem, 1, west)
    pl.when(has_east)(to_east.start)
    pl.when(has_west)(to_west.start)
    ups, downs = [], []
    at = 0
    for c, size in enumerate(up_sizes):
        part = pl.ds(at, size)
        ups.append(remote(patch_ref.at[part], from_below.at[part], (up_send, up_recv), c, above))
        at += size
    at = 0
    for c, size in enumerate(down_sizes):
        part = pl.ds(at, size)
        source = merged if c == len(down_sizes) - 1 else patch_ref.at[pl.ds(low + at, size)]
        downs.append(remote(source, from_above.at[part], (down_send, down_recv), c, below))
        at += size
    held_up, held_down = pl.ds(0, up_sizes[relay]), pl.ds(0, down_sizes[relay])
    up_source = pl.ds(sum(up_sizes[:relay]), up_sizes[relay])
    down_offset = sum(down_sizes[:relay])
    up_leg = remote_at(
        patch_ref.at[up_source], from_above.at[held_up], relay_sem, 0, {"sec": sections - 1}
    )
    down_leg = remote_at(
        patch_ref.at[pl.ds(low + down_offset, down_sizes[relay])],
        from_below.at[held_down],
        relay_sem,
        1,
        {"sec": 0},
    )
    up_on = remote(
        from_above.at[held_up], from_below.at[up_source], (up_send, up_recv), relay, {"sec": middle}
    )
    down_on = remote(
        from_below.at[held_down],
        from_above.at[pl.ds(down_offset, down_sizes[relay])],
        (down_send, down_recv),
        relay,
        {"sec": middle - 1},
    )
    pl.when(is_low)(up_leg.start)
    pl.when(is_high)(down_leg.start)
    for c in range(len(up_sizes)):
        last = c == len(up_sizes) - 1
        sends_up = has_above & ~late_up if last else has_above
        pl.when(sends_up & ~is_low if c == relay else sends_up)(ups[c].start)
        if not last:
            pl.when(has_below & ~is_high if c == relay else has_below)(downs[c].start)
    sums[...] = jnp.zeros_like(sums)
    mine[3].wait()

    @pl.when(has_below)
    def _():
        shift_copy.wait_recv()
        for j in range(rim):
            merged[j] = jnp.where(
                jnp.broadcast_to(far_shift[0:1, :], (extent, lanes)) <= j - REACH,
                local[sent - REACH - 1 + j].astype(jnp.float32),
                local[(extent - REACH + 1 + j) % extent].astype(jnp.float32),
            ).astype(jnp.bfloat16)
        build_shifted(
            shifted_up, local, temp, -1, 0, extent, far_shift[0:1, :], far_shift[1:2, :]
        )
        pl.when(~late_down)(downs[-1].start)

    @pl.when(has_above)
    def _():
        build_shifted(
            shifted_down, local, temp, sent - REACH - 2, sent, extent, -shift[0:1, :], -shift[1:2, :]
        )
        for i in range(rim + 2):
            shifted_rim[i] = shifted_down[i] + shifted_down[extent - sent + 2 + i]

    pl.when(has_west)(to_east.wait_recv)
    pl.when(has_east)(to_west.wait_recv)
    pl.when(has_east)(info_copy.wait_recv)
    lane = lax.broadcasted_iota(jnp.int32, (rows, cols), 1)
    in_east = (lane < ITERS) & has_east
    in_west = (lane >= cols - ITERS) & has_west
    for k in range(2):
        fields[k, :, :cols] = prior[k]
        between = jnp.zeros((cols - 2 * ITERS, rows), jnp.float32)
        fields[k, :, cols:] = jnp.transpose(
            jnp.concatenate([far_rims[0, k], between, far_rims[1, k]], 0)
        )
        fields[2 + k] = jnp.zeros((rows, 2 * cols), jnp.float32)
    inside = jnp.concatenate(
        [jnp.ones((rows, cols), jnp.float32), jnp.where(in_east | in_west, 1.0, 0.0)], 1
    )
    at_nodes = slot_places(
        2 * cols, lanes, cols, PCOLS,
        lambda lane: jnp.where(lane % col_step == 0, lane // col_step, -2),
    )
    both_alive = jnp.concatenate([alive, east_info[2:3, :]], 1)
    spots = jnp.dot(
        by_patch_row(both_alive, patch_rows).astype(jnp.bfloat16),
        at_nodes,
        preferred_element_type=jnp.float32,
    ).astype(jnp.bfloat16)
    spread = jnp.where(
        lax.broadcasted_iota(jnp.int32, (rows, patch_rows), 0)
        == row_step * lax.broadcasted_iota(jnp.int32, (rows, patch_rows), 1),
        1.0,
        0.0,
    ).astype(jnp.bfloat16)
    weight = jnp.dot(spread, spots, preferred_element_type=jnp.float32)
    gain[...] = (0.2 - 0.1 * weight) * inside
    wide_lane = lax.broadcasted_iota(jnp.int32, weight.shape, 1)
    for k in range(2):
        goals[k] = jnp.where(wide_lane // col_step % 2 == k, 0.4 * weight, 0.0)
    row = lax.broadcasted_iota(jnp.int32, weight.shape, 0)

    def sweep(_, carry):
        for k in range(4):
            field = fields[k]
            upper = jnp.where(row == 0, 0.0, pltpu.roll(field, 1, 0))
            lower = jnp.where(row == rows - 1, 0.0, pltpu.roll(field, rows - 1, 0))
            left = pltpu.roll(field, 1, 1)
            right = pltpu.roll(field, 2 * cols - 1, 1)
            field = 0.2 * field + gain[...] * ((upper + lower) + (left + right))
            fields[k] = field + goals[k - 2] if k >= 2 else field
        return carry

    lax.fori_loop(0, ITERS, sweep, 0)
    for k in range(4):
        base_ref[k] = fields[k, :, :cols]
    owner_ref[...] = slot_places(
        2 * cols, lanes, cols, PCOLS,
        lambda lane: jnp.where(
            lane < cols,
            2 * ((lane + col_step) // (2 * col_step)),
            2 * ((lane - cols) // (2 * col_step)) + 1,
        ),
    )

    @pl.when(is_first)
    def _():
        down_leg.wait_recv()
        down_on.start()

    @pl.when(is_last)
    def _():
        up_leg.wait_recv()
        up_on.start()

    up_at = down_at = 0
    for c, (up_size, down_size) in enumerate(zip(up_sizes, down_sizes, strict=True)):
        final = c == len(up_sizes) - 1

        @pl.when(has_below)
        def _():
            ups[c].wait_recv()
            add_lags(sums.at[0], from_below, up_at, shifted_up, up_at, up_size)

        if c == len(up_sizes) - 2:
            pl.when(has_above & late_up)(ups[-1].start)
        if final:

            @pl.when(has_below)
            def _():
                for k in range(9):
                    part_up[k : k + 1, :] = jnp.sum(sums[0, k], axis=0, keepdims=True)

            up_part = remote_at(part_up, own_up, part_sem, 0, below)
            up_part_west = remote_at(part_up, east_up, part_sem, 1, below_west)
            pl.when(has_below)(up_part.start)
            pl.when(has_below & has_west)(up_part_west.start)

        if c == relay:
            pl.when(has_below & late_down)(downs[-1].start)

        @pl.when(has_above)
        def _():
            downs[c].wait_recv()
            if final:
                add_lags(sums.at[1], from_above, down_at, shifted_rim, 0, down_size)
            else:
                add_lags(sums.at[1], from_above, down_at, shifted_down, down_at + rim, down_size)

        up_at += up_size
        down_at += down_size

    for k in range(9):
        part_down[k : k + 1, :] = jnp.sum(sums[1, 8 - k], axis=0, keepdims=True)
    down_part = remote_at(part_down, east_down, part_sem, 2, west)
    pl.when(has_west)(down_part.start)

    pl.when(has_above)(up_part.wait_recv)
    scale = float(extent)
    flow_a, flow_b = flow_lines(
        [(part_down[k : k + 1, :] + own_up[k : k + 1, :]) / scale for k in range(9)],
        row_shift,
        col_shift,
        alive,
    )
    line_ref[0:1, :] = flow_a
    line_ref[1:2, :] = flow_b
    pl.when(has_east)(down_part.wait_recv)
    pl.when(has_above & has_east)(up_part_west.wait_recv)
    east_a, east_b = flow_lines(
        [(east_down[k : k + 1, :] + east_up[k : k + 1, :]) / scale for k in range(9)],
        east_info[0:1, :],
        east_info[1:2, :],
        east_info[2:3, :],
    )
    line_ref[2:3, :] = east_a
    line_ref[3:4, :] = east_b

    pl.when(has_above)(shift_copy.wait_send)
    for c in range(len(up_sizes)):
        pl.when(has_above & ~is_low if c == relay else has_above)(ups[c].wait_send)
        pl.when(has_below & ~is_high if c == relay else has_below)(downs[c].wait_send)
    pl.when(is_low)(up_leg.wait_send)
    pl.when(is_high)(down_leg.wait_send)
    pl.when(is_first)(down_on.wait_send)
    pl.when(is_last)(up_on.wait_send)
    pl.when(has_east)(to_east.wait_send)
    pl.when(has_west)(to_west.wait_send)
    pl.when(has_west)(info_copy.wait_send)
    pl.when(has_below)(up_part.wait_send)
    pl.when(has_below & has_west)(up_part_west.wait_send)
    pl.when(has_west)(down_part.wait_send)


def finish_kernel(line_ref, base_ref, owner_ref, flow_ref, out_ref):
    rows, cols = base_ref.shape[1:]
    patch_rows = line_ref.shape[1] // PCOLS
    step = rows // patch_rows
    flow_ref[...] = line_ref[0:2, :]
    left = jnp.concatenate(
        [
            by_patch_row(
                jnp.concatenate([line_ref[k : k + 1, :], line_ref[k + 2 : k + 3, :]], 1), patch_rows
            )
            for k in range(2)
        ],
        0,
    )
    first = left.astype(jnp.bfloat16)
    rest = left - first.astype(jnp.float32)
    second = rest.astype(jnp.bfloat16)
    third = (rest - second.astype(jnp.float32)).astype(jnp.bfloat16)
    parts = jnp.dot(
        jnp.concatenate([first, second, third], 0), owner_ref[...], preferred_element_type=jnp.float32
    )
    size = 2 * patch_rows
    values = parts[:size] + parts[size : 2 * size] + parts[2 * size :]
    strip = step // 2
    for m in range(rows // strip):
        owner = (m + 1) // 2
        part = pl.ds(m * strip, strip)
        for k in range(2):
            result = base_ref[k, part, :]
            if owner < patch_rows:
                value = values[k * patch_rows + owner : k * patch_rows + owner + 1]
                result = (
                    result
                    + base_ref[2, part, :] * value[:, :cols]
                    + base_ref[3, part, :] * value[:, cols:]
                )
            out_ref[k, part, :] = result


def body(patches, counts, peak_shifts, mesh_prior):
    sections, tiles = lax.axis_size("sec"), lax.axis_size("tile")
    by_slot = jnp.transpose(patches[0], (1, 2, 0))
    extent, _, slots = by_slot.shape
    prior = mesh_prior[0, 0]
    rows, cols = prior.shape[1:]
    sent, rim = rows_up(extent), 2 * REACH
    up_sizes, down_sizes = chunk_sizes(extent)
    padded = extent + 2 * RIM
    sems = pltpu.SemaphoreType.DMA
    vmem = pl.BlockSpec(memory_space=pltpu.VMEM)
    f32, bf16 = jnp.float32, jnp.bfloat16
    lines, base, owners = pl.pallas_call(
        functools.partial(kernel, sections, tiles),
        in_specs=[pl.BlockSpec(memory_space=pltpu.HBM)] * 4,
        out_specs=[vmem, vmem, vmem],
        out_shape=[
            pltpu.VMEM((8, slots), f32),
            pltpu.VMEM((4, rows, cols), f32),
            pltpu.VMEM((2 * slots, 2 * cols), bf16),
        ],
        scratch_shapes=[
            pltpu.VMEM(by_slot.shape, bf16),
            pltpu.VMEM((rim, extent, slots), bf16),
            pltpu.VMEM((sum(down_sizes), extent, slots), bf16),
            pltpu.VMEM((sum(up_sizes), extent, slots), bf16),
            pltpu.VMEM((sent + 2, padded, slots), f32),
            pltpu.VMEM((extent - sent + 4 + rim, padded, slots), f32),
            pltpu.VMEM((rim + 2, padded, slots), f32),
            pltpu.VMEM((padded, slots), f32),
            pltpu.VMEM((2, 9, 8, slots), f32),
            pltpu.SMEM((1, 1), jnp.int32),
            pltpu.VMEM((2, slots), jnp.int32),
            pltpu.VMEM((2, slots), jnp.int32),
            pltpu.VMEM(prior.shape, f32),
            pltpu.VMEM((2, 2, ITERS, rows), f32),
            pltpu.VMEM((2, 2, ITERS, rows), f32),
            pltpu.VMEM((4, rows, 2 * cols), f32),
            pltpu.VMEM((2, rows, 2 * cols), f32),
            pltpu.VMEM((rows, 2 * cols), f32),
            pltpu.VMEM((8, slots), f32),
            pltpu.VMEM((8, slots), f32),
            pltpu.VMEM((16, slots), f32),
            pltpu.VMEM((16, slots), f32),
            pltpu.VMEM((16, slots), f32),
            pltpu.VMEM((16, slots), f32),
            pltpu.VMEM((16, slots), f32),
            sems((4,)),
            sems((len(up_sizes),)),
            sems((len(up_sizes),)),
            sems((len(down_sizes),)),
            sems((len(down_sizes),)),
            sems((2,)),
            sems((4,)),
            sems((2,)),
            sems((6,)),
            sems((4,)),
        ],
        compiler_params=pltpu.CompilerParams(collective_id=0, has_side_effects=True),
    )(by_slot, counts, peak_shifts[0], prior)
    flows, displacement = pl.pallas_call(
        finish_kernel,
        in_specs=[vmem, vmem, vmem],
        out_specs=[vmem, vmem],
        out_shape=[
            jax.ShapeDtypeStruct((2, slots), f32),
            jax.ShapeDtypeStruct(prior.shape, f32),
        ],
    )(*[pltpu.with_memory_space_constraint(x, pltpu.VMEM) for x in (lines, base, owners)])
    return flows[None], displacement[None, None]


def solution(mesh):
    placed = (
        P("sec", "tile", None, None),
        P("sec", "tile"),
        P("sec", None, "tile"),
        P("sec", "tile", None, None, None),
    )
    return jax.shard_map(
        body,
        mesh=mesh,
        in_specs=placed,
        out_specs=(P("sec", None, "tile"), P("sec", "tile", None, None, None)),
        check_vma=False,
    )
```

```python
import functools

import jax
import jax.numpy as jnp
from jax import lax
from jax.experimental import pallas as pl
from jax.experimental.pallas import tpu as pltpu
from jax.sharding import PartitionSpec as P

PCOLS = 16
ITERS = 8
REACH = 3
RIM = 8

MESH = pl.DeviceIdType.MESH


def rows_up(extent):
    return extent // 2 + 1


def chunk_sizes(extent):
    size = max(6, extent // 10)
    full = extent // 2 // size - 1
    sent = rows_up(extent)
    up = [size] * full + [sent - size * full - 4, 4]
    down = [size] * full + [extent - sent - REACH - 1 - size * full, 2 * REACH]
    return up, down


def build_shifted(dst, local, temp, base, low, high, row_shift, col_shift):
    extent = local.shape[0]
    row_shift = jnp.broadcast_to(row_shift, (extent, row_shift.shape[1]))
    col_shift = jnp.broadcast_to(col_shift, (extent, col_shift.shape[1]))

    def row(i, carry):
        total = None
        for k in range(-REACH, REACH + 1):
            at = base + i + k
            value = local[lax.rem(at + extent, extent)].astype(jnp.float32)
            if low > 0:
                value = value * jnp.where((at >= low) & (at < high), 1.0, 0.0)
            total = value if total is None else jnp.where(row_shift == k, value, total)
        temp[pl.ds(RIM, extent), :] = total
        temp[pl.ds(0, RIM), :] = total[extent - RIM :]
        temp[pl.ds(RIM + extent, RIM), :] = total[:RIM]
        total = None
        for k in range(-REACH, REACH + 1):
            value = temp[pl.ds(RIM + k, extent), :]
            total = value if total is None else jnp.where(col_shift == k, value, total)
        dst[i, pl.ds(RIM, extent), :] = total
        dst[i, pl.ds(0, RIM), :] = total[extent - RIM :]
        dst[i, pl.ds(RIM + extent, RIM), :] = total[:RIM]
        return carry

    lax.fori_loop(0, dst.shape[0], row, 0)


def add_lags(sums, other, start, shifted, first, count):
    extent, lanes = other.shape[1:]

    def row(i, totals):
        value = other[start + i].astype(jnp.float32)
        result = []
        for a in range(3):
            for b in range(3):
                product = value * shifted[first + i + a, pl.ds(RIM + b - 1, extent), :]
                total = totals[3 * a + b]
                for j in range(extent // 8):
                    total = total + product[8 * j : 8 * j + 8]
                result.append(total)
        return tuple(result)

    begun = tuple(sums[k] for k in range(9))
    for k, total in enumerate(lax.fori_loop(0, count, row, begun)):
        sums[k] = total


def slot_places(extent_lanes, lanes, cols, patch_cols, homes):
    slot = lax.broadcasted_iota(jnp.int32, (2 * lanes, extent_lanes), 0)
    lane = lax.broadcasted_iota(jnp.int32, (2 * lanes, extent_lanes), 1)
    within = slot % patch_cols
    column = jnp.where(slot < lanes, within, jnp.where(within == 0, patch_cols, -1))
    return jnp.where(column == homes(lane), 1.0, 0.0).astype(jnp.bfloat16)


def by_patch_row(line, patch_rows):
    shape = (patch_rows, line.shape[1])
    slots = patch_rows * PCOLS
    of = lax.broadcasted_iota(jnp.int32, shape, 1) % slots // PCOLS
    return jnp.where(of == lax.broadcasted_iota(jnp.int32, shape, 0), line, 0.0)


def flow_lines(scores, row_shift, col_shift, live):
    weights = [score * score for score in scores]
    total = 1.0 + sum(weights)
    row_part = (weights[6] + weights[7] + weights[8] - weights[0] - weights[1] - weights[2]) / total
    col_part = (weights[2] + weights[5] + weights[8] - weights[0] - weights[3] - weights[6]) / total
    return (
        jnp.where(live > 0.0, row_shift + row_part, 0.0),
        jnp.where(live > 0.0, col_shift + col_part, 0.0),
    )


def kernel(
    sections, tiles,
    patch_ref, count_ref, shift_ref, prior_ref,
    line_ref, base_ref, owner_ref,
    local, merged, from_above, from_below, shifted_up, shifted_down, shifted_rim, temp, sums,
    count, shift, far_shift, prior, rims, far_rims, fields, goals, gain,
    info, east_info, part_up, part_down, own_up, east_up, east_down,
    local_sem, up_send, up_recv, down_send, down_recv,
    shift_sem, rim_sem, info_sem, part_sem, relay_sem, ready,
):
    sec, tile = lax.axis_index("sec"), lax.axis_index("tile")
    extent, lanes = local.shape[1:]
    sent = rows_up(extent)
    rim = 2 * REACH
    low = sent + REACH - 1
    up_sizes, down_sizes = chunk_sizes(extent)
    rows, cols = prior.shape[1:]
    patch_rows = lanes // PCOLS
    row_step, col_step = rows // patch_rows, cols // PCOLS
    has_below, has_above = sec > 0, sec < sections - 1
    has_west, has_east = tile > 0, tile < tiles - 1
    even = lax.rem(tile, 2) == 0
    middle, relay = sections // 2, len(up_sizes) - 2
    is_low, is_high = sec == middle - 1, sec == middle
    is_first, is_last = sec == 0, sec == sections - 1
    late_up, late_down = ~even & ~is_low, ~even & ~is_high

    far_rims[...] = jnp.zeros_like(far_rims)
    line_ref[...] = jnp.zeros_like(line_ref)
    for buffer in (info, east_info, part_up, part_down, own_up, east_up, east_down):
        buffer[...] = jnp.zeros_like(buffer)

    barrier = pltpu.get_barrier_semaphore()
    below, above = {"sec": sec - 1}, {"sec": sec + 1}
    west, east = {"tile": tile - 1}, {"tile": tile + 1}
    below_west = {"sec": sec - 1, "tile": tile - 1}
    partners = [
        (has_below, below),
        (has_above, above),
        (has_west, west),
        (has_east, east),
        (is_first, {"sec": middle}),
        (is_last, {"sec": middle}),
    ]
    partners[0] = (has_below & ~is_high, below)
    greeted = [has_below, has_above & ~is_low, has_west, has_east, is_high, is_high]

    def greet(where):
        return lambda: pl.semaphore_signal(
            barrier, 1, device_id=where, device_id_type=MESH
        )

    for have, where in partners:
        pl.when(have)(greet(where))
    waits = sum(jnp.where(have, 1, 0) for have in greeted)
    mine = [
        pltpu.make_async_copy(src, dst, local_sem.at[k])
        for k, (src, dst) in enumerate(
            ((shift_ref, shift), (count_ref, count), (prior_ref, prior), (patch_ref, local))
        )
    ]
    for copy in mine:
        copy.start()
    mine[0].wait()
    mine[1].wait()
    alive = jnp.where(
        lax.broadcasted_iota(jnp.int32, (1, lanes), 1) < count[0, 0], 1.0, 0.0
    )
    row_shift = shift[0:1, :].astype(jnp.float32)
    col_shift = shift[1:2, :].astype(jnp.float32)
    info[0:1, :] = row_shift
    info[1:2, :] = col_shift
    info[2:3, :] = alive
    mine[2].wait()
    for k in range(2):
        turned = jnp.transpose(prior[k])
        rims[0, k] = turned[:ITERS]
        rims[1, k] = turned[cols - ITERS :]
    pl.semaphore_wait(barrier, waits)

    def remote(src, dst, sems, k, where):
        return pltpu.make_async_remote_copy(
            src_ref=src,
            dst_ref=dst,
            send_sem=sems[0].at[k],
            recv_sem=sems[1].at[k],
            device_id=where,
            device_id_type=MESH,
        )

    def remote_at(src, dst, sems, k, where):
        send, recv = sems.at[2 * k], sems.at[2 * k + 1]
        return pltpu.make_async_remote_copy(
            src_ref=src, dst_ref=dst, send_sem=send, recv_sem=recv, device_id=where, device_id_type=MESH
        )

    shift_copy = remote_at(shift_ref, far_shift, shift_sem, 0, above)
    pl.when(has_above & ~is_low)(shift_copy.start)
    info_copy = remote_at(info, east_info, info_sem, 0, west)
    pl.when(has_west)(info_copy.start)
    to_east = remote_at(rims.at[1], far_rims.at[1], rim_sem, 0, east)
    to_west = remote_at(rims.at[0], far_rims.at[0], rim_sem, 1, west)
    pl.when(has_east)(to_east.start)
    pl.when(has_west)(to_west.start)
    ups, downs = [], []
    at = 0
    for c, size in enumerate(up_sizes):
        part = pl.ds(at, size)
        ups.append(remote(patch_ref.at[part], from_below.at[part], (up_send, up_recv), c, above))
        at += size
    at = 0
    for c, size in enumerate(down_sizes):
        part = pl.ds(at, size)
        source = merged if c == len(down_sizes) - 1 else patch_ref.at[pl.ds(low + at, size)]
        downs.append(remote(source, from_above.at[part], (down_send, down_recv), c, below))
        at += size
    held_up, held_down = pl.ds(0, up_sizes[relay]), pl.ds(0, down_sizes[relay])
    up_source = pl.ds(sum(up_sizes[:relay]), up_sizes[relay])
    down_offset = sum(down_sizes[:relay])
    up_leg = remote_at(
        patch_ref.at[up_source], from_above.at[held_up], relay_sem, 0, {"sec": sections - 1}
    )
    down_leg = remote_at(
        patch_ref.at[pl.ds(low + down_offset, down_sizes[relay])],
        from_below.at[held_down],
        relay_sem,
        1,
        {"sec": 0},
    )
    up_on = remote(
        from_above.at[held_up], from_below.at[up_source], (up_send, up_recv), relay, {"sec": middle}
    )
    down_on = remote(
        from_below.at[held_down],
        from_above.at[pl.ds(down_offset, down_sizes[relay])],
        (down_send, down_recv),
        relay,
        {"sec": middle - 1},
    )
    pl.when(is_high)(down_leg.start)
    for c in range(len(up_sizes)):
        sends_up = has_above & ~is_low & ~late_up if c >= relay else has_above & ~is_low
        pl.when(sends_up)(ups[c].start)
        if c < len(down_sizes) - 1:
            pl.when(has_below & ~is_high if c == relay else has_below)(downs[c].start)

    @pl.when(is_high)
    def _():
        pl.semaphore_signal(ready, 1, device_id=below, device_id_type=MESH)

    @pl.when(is_low)
    def _():
        pl.semaphore_wait(ready, 1)
        shift_copy.start()
        up_leg.start()
        for c in range(len(up_sizes)):
            if c != relay:
                ups[c].start()

    sums[...] = jnp.zeros_like(sums)
    mine[3].wait()

    @pl.when(has_below)
    def _():
        shift_copy.wait_recv()
        for j in range(rim):
            merged[j] = jnp.where(
                jnp.broadcast_to(far_shift[0:1, :], (extent, lanes)) <= j - REACH,
                local[sent - REACH - 1 + j].astype(jnp.float32),
                local[(extent - REACH + 1 + j) % extent].astype(jnp.float32),
            ).astype(jnp.bfloat16)
        build_shifted(
            shifted_up, local, temp, -1, 0, extent, far_shift[0:1, :], far_shift[1:2, :]
        )
        pl.when(~late_down)(downs[-1].start)

    @pl.when(has_above)
    def _():
        build_shifted(
            shifted_down, local, temp, sent - REACH - 2, sent, extent, -shift[0:1, :], -shift[1:2, :]
        )
        for i in range(rim + 2):
            shifted_rim[i] = shifted_down[i] + shifted_down[extent - sent + 2 + i]

    pl.when(has_west)(to_east.wait_recv)
    pl.when(has_east)(to_west.wait_recv)
    pl.when(has_east)(info_copy.wait_recv)
    lane = lax.broadcasted_iota(jnp.int32, (rows, cols), 1)
    in_east = (lane < ITERS) & has_east
    in_west = (lane >= cols - ITERS) & has_west
    for k in range(2):
        fields[k, :, :cols] = prior[k]
        between = jnp.zeros((cols - 2 * ITERS, rows), jnp.float32)
        fields[k, :, cols:] = jnp.transpose(
            jnp.concatenate([far_rims[0, k], between, far_rims[1, k]], 0)
        )
        fields[2 + k] = jnp.zeros((rows, 2 * cols), jnp.float32)
    inside = jnp.concatenate(
        [jnp.ones((rows, cols), jnp.float32), jnp.where(in_east | in_west, 1.0, 0.0)], 1
    )
    at_nodes = slot_places(
        2 * cols, lanes, cols, PCOLS,
        lambda lane: jnp.where(lane % col_step == 0, lane // col_step, -2),
    )
    both_alive = jnp.concatenate([alive, east_info[2:3, :]], 1)
    spots = jnp.dot(
        by_patch_row(both_alive, patch_rows).astype(jnp.bfloat16),
        at_nodes,
        preferred_element_type=jnp.float32,
    ).astype(jnp.bfloat16)
    spread = jnp.where(
        lax.broadcasted_iota(jnp.int32, (rows, patch_rows), 0)
        == row_step * lax.broadcasted_iota(jnp.int32, (rows, patch_rows), 1),
        1.0,
        0.0,
    ).astype(jnp.bfloat16)
    weight = jnp.dot(spread, spots, preferred_element_type=jnp.float32)
    gain[...] = (0.2 - 0.1 * weight) * inside
    wide_lane = lax.broadcasted_iota(jnp.int32, weight.shape, 1)
    for k in range(2):
        goals[k] = jnp.where(wide_lane // col_step % 2 == k, 0.4 * weight, 0.0)
    row = lax.broadcasted_iota(jnp.int32, weight.shape, 0)

    def sweep(_, carry):
        for k in range(4):
            field = fields[k]
            upper = jnp.where(row == 0, 0.0, pltpu.roll(field, 1, 0))
            lower = jnp.where(row == rows - 1, 0.0, pltpu.roll(field, rows - 1, 0))
            left = pltpu.roll(field, 1, 1)
            right = pltpu.roll(field, 2 * cols - 1, 1)
            field = 0.2 * field + gain[...] * ((upper + lower) + (left + right))
            fields[k] = field + goals[k - 2] if k >= 2 else field
        return carry

    lax.fori_loop(0, ITERS, sweep, 0)
    for k in range(4):
        base_ref[k] = fields[k, :, :cols]
    owner_ref[...] = slot_places(
        2 * cols, lanes, cols, PCOLS,
        lambda lane: jnp.where(
            lane < cols,
            2 * ((lane + col_step) // (2 * col_step)),
            2 * ((lane - cols) // (2 * col_step)) + 1,
        ),
    )

    @pl.when(is_first)
    def _():
        down_leg.wait_recv()
        down_on.start()

    @pl.when(is_last)
    def _():
        up_leg.wait_recv()
        up_on.start()

    up_part = remote_at(part_up, own_up, part_sem, 0, below)
    up_part_west = remote_at(part_up, east_up, part_sem, 1, below_west)

    def take_up(c):
        at, size = sum(up_sizes[:c]), up_sizes[c]

        @pl.when(has_below)
        def _():
            ups[c].wait_recv()
            add_lags(sums.at[0], from_below, at, shifted_up, at, size)

    def take_down(c):
        at, size = sum(down_sizes[:c]), down_sizes[c]
        pl.when(has_above)(downs[c].wait_recv)
        if c == relay:
            pl.when(has_below & late_down & ~is_low)(downs[-1].start)

        @pl.when(has_above)
        def _():
            if c == len(down_sizes) - 1:
                add_lags(sums.at[1], from_above, at, shifted_rim, 0, size)
            else:
                add_lags(sums.at[1], from_above, at, shifted_down, at + rim, size)

    for c in range(relay):
        take_up(c)
        take_down(c)
    pl.when(has_above & late_up)(ups[relay].start)
    pl.when(has_above & late_up)(ups[-1].start)
    take_down(relay)

    @pl.when(late_down & is_low)
    def _():
        downs[relay].wait_send()
        downs[-1].start()

    take_up(relay)
    take_up(relay + 1)

    @pl.when(has_below)
    def _():
        for k in range(9):
            part_up[k : k + 1, :] = jnp.sum(sums[0, k], axis=0, keepdims=True)

    pl.when(has_below & has_west)(up_part_west.start)
    pl.when(has_below)(up_part.start)
    take_down(relay + 1)

    for k in range(9):
        part_down[k : k + 1, :] = jnp.sum(sums[1, 8 - k], axis=0, keepdims=True)
    down_part = remote_at(part_down, east_down, part_sem, 2, west)
    pl.when(has_west)(down_part.start)

    pl.when(has_above)(up_part.wait_recv)
    scale = float(extent)
    flow_a, flow_b = flow_lines(
        [(part_down[k : k + 1, :] + own_up[k : k + 1, :]) / scale for k in range(9)],
        row_shift,
        col_shift,
        alive,
    )
    line_ref[0:1, :] = flow_a
    line_ref[1:2, :] = flow_b
    pl.when(has_east)(down_part.wait_recv)
    pl.when(has_above & has_east)(up_part_west.wait_recv)
    east_a, east_b = flow_lines(
        [(east_down[k : k + 1, :] + east_up[k : k + 1, :]) / scale for k in range(9)],
        east_info[0:1, :],
        east_info[1:2, :],
        east_info[2:3, :],
    )
    line_ref[2:3, :] = east_a
    line_ref[3:4, :] = east_b

    pl.when(has_above)(shift_copy.wait_send)
    for c in range(len(up_sizes)):
        pl.when(has_above & ~is_low if c == relay else has_above)(ups[c].wait_send)
        sent_down = has_below & ~is_high & ~(late_down & is_low) if c == relay else has_below
        pl.when(sent_down)(downs[c].wait_send)
    pl.when(is_low)(up_leg.wait_send)
    pl.when(is_high)(down_leg.wait_send)
    pl.when(is_first)(down_on.wait_send)
    pl.when(is_last)(up_on.wait_send)
    pl.when(has_east)(to_east.wait_send)
    pl.when(has_west)(to_west.wait_send)
    pl.when(has_west)(info_copy.wait_send)
    pl.when(has_below)(up_part.wait_send)
    pl.when(has_below & has_west)(up_part_west.wait_send)
    pl.when(has_west)(down_part.wait_send)


def finish_kernel(line_ref, base_ref, owner_ref, flow_ref, out_ref):
    rows, cols = base_ref.shape[1:]
    patch_rows = line_ref.shape[1] // PCOLS
    step = rows // patch_rows
    flow_ref[...] = line_ref[0:2, :]
    left = jnp.concatenate(
        [
            by_patch_row(
                jnp.concatenate([line_ref[k : k + 1, :], line_ref[k + 2 : k + 3, :]], 1), patch_rows
            )
            for k in range(2)
        ],
        0,
    )
    first = left.astype(jnp.bfloat16)
    rest = left - first.astype(jnp.float32)
    second = rest.astype(jnp.bfloat16)
    third = (rest - second.astype(jnp.float32)).astype(jnp.bfloat16)
    parts = jnp.dot(
        jnp.concatenate([first, second, third], 0), owner_ref[...], preferred_element_type=jnp.float32
    )
    size = 2 * patch_rows
    values = parts[:size] + parts[size : 2 * size] + parts[2 * size :]
    strip = step // 2
    for m in range(rows // strip):
        owner = (m + 1) // 2
        part = pl.ds(m * strip, strip)
        for k in range(2):
            result = base_ref[k, part, :]
            if owner < patch_rows:
                value = values[k * patch_rows + owner : k * patch_rows + owner + 1]
                result = (
                    result
                    + base_ref[2, part, :] * value[:, :cols]
                    + base_ref[3, part, :] * value[:, cols:]
                )
            out_ref[k, part, :] = result


def body(patches, counts, peak_shifts, mesh_prior):
    sections, tiles = lax.axis_size("sec"), lax.axis_size("tile")
    by_slot = jnp.transpose(patches[0], (1, 2, 0))
    extent, _, slots = by_slot.shape
    prior = mesh_prior[0, 0]
    rows, cols = prior.shape[1:]
    sent, rim = rows_up(extent), 2 * REACH
    up_sizes, down_sizes = chunk_sizes(extent)
    padded = extent + 2 * RIM
    sems = pltpu.SemaphoreType.DMA
    vmem = pl.BlockSpec(memory_space=pltpu.VMEM)
    f32, bf16 = jnp.float32, jnp.bfloat16
    lines, base, owners = pl.pallas_call(
        functools.partial(kernel, sections, tiles),
        in_specs=[pl.BlockSpec(memory_space=pltpu.HBM)] * 4,
        out_specs=[vmem, vmem, vmem],
        out_shape=[
            pltpu.VMEM((8, slots), f32),
            pltpu.VMEM((4, rows, cols), f32),
            pltpu.VMEM((2 * slots, 2 * cols), bf16),
        ],
        scratch_shapes=[
            pltpu.VMEM(by_slot.shape, bf16),
            pltpu.VMEM((rim, extent, slots), bf16),
            pltpu.VMEM((sum(down_sizes), extent, slots), bf16),
            pltpu.VMEM((sum(up_sizes), extent, slots), bf16),
            pltpu.VMEM((sent + 2, padded, slots), f32),
            pltpu.VMEM((extent - sent + 4 + rim, padded, slots), f32),
            pltpu.VMEM((rim + 2, padded, slots), f32),
            pltpu.VMEM((padded, slots), f32),
            pltpu.VMEM((2, 9, 8, slots), f32),
            pltpu.SMEM((1, 1), jnp.int32),
            pltpu.VMEM((2, slots), jnp.int32),
            pltpu.VMEM((2, slots), jnp.int32),
            pltpu.VMEM(prior.shape, f32),
            pltpu.VMEM((2, 2, ITERS, rows), f32),
            pltpu.VMEM((2, 2, ITERS, rows), f32),
            pltpu.VMEM((4, rows, 2 * cols), f32),
            pltpu.VMEM((2, rows, 2 * cols), f32),
            pltpu.VMEM((rows, 2 * cols), f32),
            pltpu.VMEM((8, slots), f32),
            pltpu.VMEM((8, slots), f32),
            pltpu.VMEM((16, slots), f32),
            pltpu.VMEM((16, slots), f32),
            pltpu.VMEM((16, slots), f32),
            pltpu.VMEM((16, slots), f32),
            pltpu.VMEM((16, slots), f32),
            sems((4,)),
            sems((len(up_sizes),)),
            sems((len(up_sizes),)),
            sems((len(down_sizes),)),
            sems((len(down_sizes),)),
            sems((2,)),
            sems((4,)),
            sems((2,)),
            sems((6,)),
            sems((4,)),
            pltpu.SemaphoreType.REGULAR,
        ],
        compiler_params=pltpu.CompilerParams(collective_id=0, has_side_effects=True),
    )(by_slot, counts, peak_shifts[0], prior)
    flows, displacement = pl.pallas_call(
        finish_kernel,
        in_specs=[vmem, vmem, vmem],
        out_specs=[vmem, vmem],
        out_shape=[
            jax.ShapeDtypeStruct((2, slots), f32),
            jax.ShapeDtypeStruct(prior.shape, f32),
        ],
    )(*[pltpu.with_memory_space_constraint(x, pltpu.VMEM) for x in (lines, base, owners)])
    return flows[None], displacement[None, None]


def solution(mesh):
    placed = (
        P("sec", "tile", None, None),
        P("sec", "tile"),
        P("sec", None, "tile"),
        P("sec", "tile", None, None, None),
    )
    return jax.shard_map(
        body,
        mesh=mesh,
        in_specs=placed,
        out_specs=(P("sec", None, "tile"), P("sec", "tile", None, None, None)),
        check_vma=False,
    )
```

```python
import functools

import jax
import jax.numpy as jnp
from jax import lax
from jax.experimental import pallas as pl
from jax.experimental.pallas import tpu as pltpu
from jax.sharding import PartitionSpec as P

PCOLS = 16
ITERS = 8
REACH = 3
RIM = 8

MESH = pl.DeviceIdType.MESH


def rows_up(extent):
    return extent // 2 + 1


def chunk_sizes(extent):
    size = max(6, extent // 10)
    full = extent // 2 // size - 1
    sent = rows_up(extent)
    up = [size] * full + [sent - size * full - 4, 4]
    down = [size] * full + [extent - sent - REACH - 1 - size * full, 2 * REACH]
    return up, down


def build_shifted(dst, local, temp, base, low, high, row_shift, col_shift):
    extent = local.shape[0]
    row_shift = jnp.broadcast_to(row_shift, (extent, row_shift.shape[1]))
    col_shift = jnp.broadcast_to(col_shift, (extent, col_shift.shape[1]))

    def row(i, carry):
        total = None
        for k in range(-REACH, REACH + 1):
            at = base + i + k
            value = local[lax.rem(at + extent, extent)].astype(jnp.float32)
            if low > 0:
                value = value * jnp.where((at >= low) & (at < high), 1.0, 0.0)
            total = value if total is None else jnp.where(row_shift == k, value, total)
        temp[pl.ds(RIM, extent), :] = total
        temp[pl.ds(0, RIM), :] = total[extent - RIM :]
        temp[pl.ds(RIM + extent, RIM), :] = total[:RIM]
        total = None
        for k in range(-REACH, REACH + 1):
            value = temp[pl.ds(RIM + k, extent), :]
            total = value if total is None else jnp.where(col_shift == k, value, total)
        dst[i, pl.ds(RIM, extent), :] = total
        dst[i, pl.ds(0, RIM), :] = total[extent - RIM :]
        dst[i, pl.ds(RIM + extent, RIM), :] = total[:RIM]
        return carry

    lax.fori_loop(0, dst.shape[0], row, 0)


def add_lags(sums, other, start, shifted, first, count):
    extent, lanes = other.shape[1:]

    def row(i, totals):
        value = other[start + i].astype(jnp.float32)
        result = []
        for a in range(3):
            for b in range(3):
                product = value * shifted[first + i + a, pl.ds(RIM + b - 1, extent), :]
                total = totals[3 * a + b]
                for j in range(extent // 8):
                    total = total + product[8 * j : 8 * j + 8]
                result.append(total)
        return tuple(result)

    begun = tuple(sums[k] for k in range(9))
    for k, total in enumerate(lax.fori_loop(0, count, row, begun)):
        sums[k] = total


def slot_places(extent_lanes, lanes, cols, patch_cols, homes):
    slot = lax.broadcasted_iota(jnp.int32, (2 * lanes, extent_lanes), 0)
    lane = lax.broadcasted_iota(jnp.int32, (2 * lanes, extent_lanes), 1)
    within = slot % patch_cols
    column = jnp.where(slot < lanes, within, jnp.where(within == 0, patch_cols, -1))
    return jnp.where(column == homes(lane), 1.0, 0.0).astype(jnp.bfloat16)


def by_patch_row(line, patch_rows):
    shape = (patch_rows, line.shape[1])
    slots = patch_rows * PCOLS
    of = lax.broadcasted_iota(jnp.int32, shape, 1) % slots // PCOLS
    return jnp.where(of == lax.broadcasted_iota(jnp.int32, shape, 0), line, 0.0)


def flow_lines(scores, row_shift, col_shift, live):
    weights = [score * score for score in scores]
    total = 1.0 + sum(weights)
    row_part = (weights[6] + weights[7] + weights[8] - weights[0] - weights[1] - weights[2]) / total
    col_part = (weights[2] + weights[5] + weights[8] - weights[0] - weights[3] - weights[6]) / total
    return (
        jnp.where(live > 0.0, row_shift + row_part, 0.0),
        jnp.where(live > 0.0, col_shift + col_part, 0.0),
    )


def kernel(
    sections, tiles,
    patch_ref, count_ref, shift_ref, prior_ref,
    line_ref, base_ref,
    local, merged, from_above, from_below, shifted_up, shifted_down, shifted_rim, temp, sums,
    count, shift, far_shift, prior, rims, far_rims, fields, goals, gain,
    info, east_info, part_up, part_down, own_up, east_up, east_down,
    local_sem, up_send, up_recv, down_send, down_recv,
    shift_sem, rim_sem, info_sem, part_sem, relay_sem, ready,
):
    sec, tile = lax.axis_index("sec"), lax.axis_index("tile")
    extent, lanes = local.shape[1:]
    sent = rows_up(extent)
    rim = 2 * REACH
    low = sent + REACH - 1
    up_sizes, down_sizes = chunk_sizes(extent)
    rows, cols = prior.shape[1:]
    patch_rows = lanes // PCOLS
    row_step, col_step = rows // patch_rows, cols // PCOLS
    has_below, has_above = sec > 0, sec < sections - 1
    has_west, has_east = tile > 0, tile < tiles - 1
    even = lax.rem(tile, 2) == 0
    middle, relay = sections // 2, len(up_sizes) - 2
    is_low, is_high = sec == middle - 1, sec == middle
    is_first, is_last = sec == 0, sec == sections - 1
    late_up, late_down = ~even & ~is_low, ~even & ~is_high
    own_pace = is_low | is_last

    far_rims[...] = jnp.zeros_like(far_rims)
    line_ref[...] = jnp.zeros_like(line_ref)
    for buffer in (info, east_info, part_up, part_down, own_up, east_up, east_down):
        buffer[...] = jnp.zeros_like(buffer)

    barrier = pltpu.get_barrier_semaphore()
    below, above = {"sec": sec - 1}, {"sec": sec + 1}
    west, east = {"tile": tile - 1}, {"tile": tile + 1}
    below_west = {"sec": sec - 1, "tile": tile - 1}
    partners = [
        (has_below, below),
        (has_above, above),
        (has_west, west),
        (has_east, east),
        (is_first, {"sec": middle}),
        (is_last, {"sec": middle}),
    ]
    partners[0] = (has_below & ~is_high, below)
    greeted = [has_below, has_above & ~is_low, has_west, has_east, is_high, is_high]

    def greet(where):
        return lambda: pl.semaphore_signal(
            barrier, 1, device_id=where, device_id_type=MESH
        )

    for have, where in partners:
        pl.when(have)(greet(where))
    waits = sum(jnp.where(have, 1, 0) for have in greeted)
    mine = [
        pltpu.make_async_copy(src, dst, local_sem.at[k])
        for k, (src, dst) in enumerate(
            ((shift_ref, shift), (count_ref, count), (prior_ref, prior), (patch_ref, local))
        )
    ]
    for copy in mine:
        copy.start()
    mine[0].wait()
    mine[1].wait()
    alive = jnp.where(
        lax.broadcasted_iota(jnp.int32, (1, lanes), 1) < count[0, 0], 1.0, 0.0
    )
    row_shift = shift[0:1, :].astype(jnp.float32)
    col_shift = shift[1:2, :].astype(jnp.float32)
    info[0:1, :] = row_shift
    info[1:2, :] = col_shift
    info[2:3, :] = alive
    mine[2].wait()
    for k in range(2):
        turned = jnp.transpose(prior[k])
        rims[0, k] = turned[:ITERS]
        rims[1, k] = turned[cols - ITERS :]
    pl.semaphore_wait(barrier, waits)

    def remote(src, dst, sems, k, where):
        return pltpu.make_async_remote_copy(
            src_ref=src,
            dst_ref=dst,
            send_sem=sems[0].at[k],
            recv_sem=sems[1].at[k],
            device_id=where,
            device_id_type=MESH,
        )

    def remote_at(src, dst, sems, k, where):
        send, recv = sems.at[2 * k], sems.at[2 * k + 1]
        return pltpu.make_async_remote_copy(
            src_ref=src, dst_ref=dst, send_sem=send, recv_sem=recv, device_id=where, device_id_type=MESH
        )

    shift_copy = remote_at(shift_ref, far_shift, shift_sem, 0, above)
    pl.when(has_above & ~is_low)(shift_copy.start)
    info_copy = remote_at(info, east_info, info_sem, 0, west)
    pl.when(has_west)(info_copy.start)
    to_east = remote_at(rims.at[1], far_rims.at[1], rim_sem, 0, east)
    to_west = remote_at(rims.at[0], far_rims.at[0], rim_sem, 1, west)
    pl.when(has_east)(to_east.start)
    pl.when(has_west)(to_west.start)
    ups, downs = [], []
    at = 0
    for c, size in enumerate(up_sizes):
        part = pl.ds(at, size)
        ups.append(remote(patch_ref.at[part], from_below.at[part], (up_send, up_recv), c, above))
        at += size
    at = 0
    for c, size in enumerate(down_sizes):
        part = pl.ds(at, size)
        source = merged if c == len(down_sizes) - 1 else patch_ref.at[pl.ds(low + at, size)]
        downs.append(remote(source, from_above.at[part], (down_send, down_recv), c, below))
        at += size
    held_up, held_down = pl.ds(0, up_sizes[relay]), pl.ds(0, down_sizes[relay])
    up_source = pl.ds(sum(up_sizes[:relay]), up_sizes[relay])
    down_offset = sum(down_sizes[:relay])
    up_leg = remote_at(
        patch_ref.at[up_source], from_above.at[held_up], relay_sem, 0, {"sec": sections - 1}
    )
    down_leg = remote_at(
        patch_ref.at[pl.ds(low + down_offset, down_sizes[relay])],
        from_below.at[held_down],
        relay_sem,
        1,
        {"sec": 0},
    )
    up_on = remote(
        from_above.at[held_up], from_below.at[up_source], (up_send, up_recv), relay, {"sec": middle}
    )
    down_on = remote(
        from_below.at[held_down],
        from_above.at[pl.ds(down_offset, down_sizes[relay])],
        (down_send, down_recv),
        relay,
        {"sec": middle - 1},
    )
    pl.when(is_high)(down_leg.start)
    for c in range(len(up_sizes)):
        sends_up = has_above & ~is_low & ~late_up if c >= relay else has_above & ~is_low
        pl.when(sends_up)(ups[c].start)
        if c < len(down_sizes) - 1:
            pl.when(has_below & ~is_high if c == relay else has_below)(downs[c].start)

    @pl.when(is_high)
    def _():
        pl.semaphore_signal(ready, 1, device_id=below, device_id_type=MESH)

    @pl.when(is_low)
    def _():
        pl.semaphore_wait(ready, 1)
        shift_copy.start()
        up_leg.start()
        for c in range(len(up_sizes)):
            if c != relay:
                ups[c].start()

    sums[...] = jnp.zeros_like(sums)
    mine[3].wait()

    @pl.when(has_below)
    def _():
        shift_copy.wait_recv()
        for j in range(rim):
            merged[j] = jnp.where(
                jnp.broadcast_to(far_shift[0:1, :], (extent, lanes)) <= j - REACH,
                local[sent - REACH - 1 + j].astype(jnp.float32),
                local[(extent - REACH + 1 + j) % extent].astype(jnp.float32),
            ).astype(jnp.bfloat16)
        build_shifted(
            shifted_up, local, temp, -1, 0, extent, far_shift[0:1, :], far_shift[1:2, :]
        )
        pl.when(~late_down)(downs[-1].start)

    @pl.when(has_above)
    def _():
        build_shifted(
            shifted_down, local, temp, sent - REACH - 2, sent, extent, -shift[0:1, :], -shift[1:2, :]
        )
        for i in range(rim + 2):
            shifted_rim[i] = shifted_down[i] + shifted_down[extent - sent + 2 + i]

    pl.when(has_west)(to_east.wait_recv)
    pl.when(has_east)(to_west.wait_recv)
    pl.when(has_east)(info_copy.wait_recv)
    lane = lax.broadcasted_iota(jnp.int32, (rows, cols), 1)
    in_east = (lane < ITERS) & has_east
    in_west = (lane >= cols - ITERS) & has_west
    for k in range(2):
        fields[k, :, :cols] = prior[k]
        between = jnp.zeros((cols - 2 * ITERS, rows), jnp.float32)
        fields[k, :, cols:] = jnp.transpose(
            jnp.concatenate([far_rims[0, k], between, far_rims[1, k]], 0)
        )
        fields[2 + k] = jnp.zeros((rows, 2 * cols), jnp.float32)
    inside = jnp.concatenate(
        [jnp.ones((rows, cols), jnp.float32), jnp.where(in_east | in_west, 1.0, 0.0)], 1
    )
    at_nodes = slot_places(
        2 * cols, lanes, cols, PCOLS,
        lambda lane: jnp.where(lane % col_step == 0, lane // col_step, -2),
    )
    both_alive = jnp.concatenate([alive, east_info[2:3, :]], 1)
    spots = jnp.dot(
        by_patch_row(both_alive, patch_rows).astype(jnp.bfloat16),
        at_nodes,
        preferred_element_type=jnp.float32,
    ).astype(jnp.bfloat16)
    spread = jnp.where(
        lax.broadcasted_iota(jnp.int32, (rows, patch_rows), 0)
        == row_step * lax.broadcasted_iota(jnp.int32, (rows, patch_rows), 1),
        1.0,
        0.0,
    ).astype(jnp.bfloat16)
    weight = jnp.dot(spread, spots, preferred_element_type=jnp.float32)
    gain[...] = (0.2 - 0.1 * weight) * inside
    wide_lane = lax.broadcasted_iota(jnp.int32, weight.shape, 1)
    for k in range(2):
        goals[k] = jnp.where(wide_lane // col_step % 2 == k, 0.4 * weight, 0.0)
    row = lax.broadcasted_iota(jnp.int32, weight.shape, 0)

    def sweep(_, carry):
        for k in range(4):
            field = fields[k]
            upper = jnp.where(row == 0, 0.0, pltpu.roll(field, 1, 0))
            lower = jnp.where(row == rows - 1, 0.0, pltpu.roll(field, rows - 1, 0))
            left = pltpu.roll(field, 1, 1)
            right = pltpu.roll(field, 2 * cols - 1, 1)
            field = 0.2 * field + gain[...] * ((upper + lower) + (left + right))
            fields[k] = field + goals[k - 2] if k >= 2 else field
        return carry

    lax.fori_loop(0, ITERS, sweep, 0)
    for k in range(4):
        base_ref[k] = fields[k, :, :cols]
    @pl.when(is_first)
    def _():
        down_leg.wait_recv()
        down_on.start()

    @pl.when(is_last)
    def _():
        up_leg.wait_recv()
        up_on.start()

    up_part = remote_at(part_up, own_up, part_sem, 0, below)
    up_part_west = remote_at(part_up, east_up, part_sem, 1, below_west)

    def take_up(c):
        at, size = sum(up_sizes[:c]), up_sizes[c]

        @pl.when(has_below)
        def _():
            ups[c].wait_recv()
            add_lags(sums.at[0], from_below, at, shifted_up, at, size)

    def take_down(c):
        at, size = sum(down_sizes[:c]), down_sizes[c]
        pl.when(has_above)(downs[c].wait_recv)
        if c == relay:
            pl.when(late_down & ~own_pace & has_below)(downs[-1].start)

        @pl.when(has_above)
        def _():
            if c == len(down_sizes) - 1:
                add_lags(sums.at[1], from_above, at, shifted_rim, 0, size)
            else:
                add_lags(sums.at[1], from_above, at, shifted_down, at + rim, size)

    for c in range(relay):
        take_up(c)
        take_down(c)
    pl.when(has_above & late_up)(ups[relay].start)
    pl.when(has_above & late_up)(ups[-1].start)
    take_down(relay)

    @pl.when(late_down & own_pace)
    def _():
        downs[relay].wait_send()
        downs[-1].start()

    take_up(relay)
    take_up(relay + 1)

    @pl.when(has_below)
    def _():
        for k in range(9):
            part_up[k : k + 1, :] = jnp.sum(sums[0, k], axis=0, keepdims=True)

    pl.when(has_below & has_west)(up_part_west.start)
    pl.when(has_below)(up_part.start)
    take_down(relay + 1)

    for k in range(9):
        part_down[k : k + 1, :] = jnp.sum(sums[1, 8 - k], axis=0, keepdims=True)
    down_part = remote_at(part_down, east_down, part_sem, 2, west)
    pl.when(has_west)(down_part.start)

    pl.when(has_above)(up_part.wait_recv)
    scale = float(extent)
    flow_a, flow_b = flow_lines(
        [(part_down[k : k + 1, :] + own_up[k : k + 1, :]) / scale for k in range(9)],
        row_shift,
        col_shift,
        alive,
    )
    line_ref[0:1, :] = flow_a
    line_ref[1:2, :] = flow_b
    pl.when(has_east)(down_part.wait_recv)
    pl.when(has_above & has_east)(up_part_west.wait_recv)
    east_a, east_b = flow_lines(
        [(east_down[k : k + 1, :] + east_up[k : k + 1, :]) / scale for k in range(9)],
        east_info[0:1, :],
        east_info[1:2, :],
        east_info[2:3, :],
    )
    line_ref[2:3, :] = east_a
    line_ref[3:4, :] = east_b

    pl.when(has_above)(shift_copy.wait_send)
    for c in range(len(up_sizes)):
        pl.when(has_above & ~is_low if c == relay else has_above)(ups[c].wait_send)
        sent_down = has_below & ~is_high & ~(late_down & own_pace) if c == relay else has_below
        pl.when(sent_down)(downs[c].wait_send)
    pl.when(is_low)(up_leg.wait_send)
    pl.when(is_high)(down_leg.wait_send)
    pl.when(is_first)(down_on.wait_send)
    pl.when(is_last)(up_on.wait_send)
    pl.when(has_east)(to_east.wait_send)
    pl.when(has_west)(to_west.wait_send)
    pl.when(has_west)(info_copy.wait_send)
    pl.when(has_below)(up_part.wait_send)
    pl.when(has_below & has_west)(up_part_west.wait_send)
    pl.when(has_west)(down_part.wait_send)


def finish_kernel(line_ref, base_ref, flow_ref, out_ref):
    rows, cols = base_ref.shape[1:]
    lanes = line_ref.shape[1]
    patch_rows, col_step = lanes // PCOLS, cols // PCOLS
    owners = slot_places(
        2 * cols, lanes, cols, PCOLS,
        lambda lane: jnp.where(
            lane < cols,
            2 * ((lane + col_step) // (2 * col_step)),
            2 * ((lane - cols) // (2 * col_step)) + 1,
        ),
    )

    step = rows // patch_rows
    flow_ref[...] = line_ref[0:2, :]
    left = jnp.concatenate(
        [
            by_patch_row(
                jnp.concatenate([line_ref[k : k + 1, :], line_ref[k + 2 : k + 3, :]], 1), patch_rows
            )
            for k in range(2)
        ],
        0,
    )
    first = left.astype(jnp.bfloat16)
    rest = left - first.astype(jnp.float32)
    second = rest.astype(jnp.bfloat16)
    third = (rest - second.astype(jnp.float32)).astype(jnp.bfloat16)
    parts = jnp.dot(
        jnp.concatenate([first, second, third], 0), owners, preferred_element_type=jnp.float32
    )
    size = 2 * patch_rows
    values = parts[:size] + parts[size : 2 * size] + parts[2 * size :]
    strip = step // 2
    for m in range(rows // strip):
        owner = (m + 1) // 2
        part = pl.ds(m * strip, strip)
        for k in range(2):
            result = base_ref[k, part, :]
            if owner < patch_rows:
                value = values[k * patch_rows + owner : k * patch_rows + owner + 1]
                result = (
                    result
                    + base_ref[2, part, :] * value[:, :cols]
                    + base_ref[3, part, :] * value[:, cols:]
                )
            out_ref[k, part, :] = result


def body(patches, counts, peak_shifts, mesh_prior):
    sections, tiles = lax.axis_size("sec"), lax.axis_size("tile")
    by_slot = jnp.transpose(patches[0], (1, 2, 0))
    extent, _, slots = by_slot.shape
    prior = mesh_prior[0, 0]
    rows, cols = prior.shape[1:]
    sent, rim = rows_up(extent), 2 * REACH
    up_sizes, down_sizes = chunk_sizes(extent)
    padded = extent + 2 * RIM
    sems = pltpu.SemaphoreType.DMA
    vmem = pl.BlockSpec(memory_space=pltpu.VMEM)
    f32, bf16 = jnp.float32, jnp.bfloat16
    lines, base = pl.pallas_call(
        functools.partial(kernel, sections, tiles),
        in_specs=[pl.BlockSpec(memory_space=pltpu.HBM)] * 4,
        out_specs=[vmem, vmem],
        out_shape=[
            pltpu.VMEM((8, slots), f32),
            pltpu.VMEM((4, rows, cols), f32),
        ],
        scratch_shapes=[
            pltpu.VMEM(by_slot.shape, bf16),
            pltpu.VMEM((rim, extent, slots), bf16),
            pltpu.VMEM((sum(down_sizes), extent, slots), bf16),
            pltpu.VMEM((sum(up_sizes), extent, slots), bf16),
            pltpu.VMEM((sent + 2, padded, slots), f32),
            pltpu.VMEM((extent - sent + 4 + rim, padded, slots), f32),
            pltpu.VMEM((rim + 2, padded, slots), f32),
            pltpu.VMEM((padded, slots), f32),
            pltpu.VMEM((2, 9, 8, slots), f32),
            pltpu.SMEM((1, 1), jnp.int32),
            pltpu.VMEM((2, slots), jnp.int32),
            pltpu.VMEM((2, slots), jnp.int32),
            pltpu.VMEM(prior.shape, f32),
            pltpu.VMEM((2, 2, ITERS, rows), f32),
            pltpu.VMEM((2, 2, ITERS, rows), f32),
            pltpu.VMEM((4, rows, 2 * cols), f32),
            pltpu.VMEM((2, rows, 2 * cols), f32),
            pltpu.VMEM((rows, 2 * cols), f32),
            pltpu.VMEM((8, slots), f32),
            pltpu.VMEM((8, slots), f32),
            pltpu.VMEM((16, slots), f32),
            pltpu.VMEM((16, slots), f32),
            pltpu.VMEM((16, slots), f32),
            pltpu.VMEM((16, slots), f32),
            pltpu.VMEM((16, slots), f32),
            sems((4,)),
            sems((len(up_sizes),)),
            sems((len(up_sizes),)),
            sems((len(down_sizes),)),
            sems((len(down_sizes),)),
            sems((2,)),
            sems((4,)),
            sems((2,)),
            sems((6,)),
            sems((4,)),
            pltpu.SemaphoreType.REGULAR,
        ],
        compiler_params=pltpu.CompilerParams(collective_id=0, has_side_effects=True),
    )(by_slot, counts, peak_shifts[0], prior)
    flows, displacement = pl.pallas_call(
        finish_kernel,
        in_specs=[vmem, vmem],
        out_specs=[vmem, vmem],
        out_shape=[
            jax.ShapeDtypeStruct((2, slots), f32),
            jax.ShapeDtypeStruct(prior.shape, f32),
        ],
    )(*[pltpu.with_memory_space_constraint(x, pltpu.VMEM) for x in (lines, base)])
    return flows[None], displacement[None, None]


def solution(mesh):
    placed = (
        P("sec", "tile", None, None),
        P("sec", "tile"),
        P("sec", None, "tile"),
        P("sec", "tile", None, None, None),
    )
    return jax.shard_map(
        body,
        mesh=mesh,
        in_specs=placed,
        out_specs=(P("sec", None, "tile"), P("sec", "tile", None, None, None)),
        check_vma=False,
    )
```

```python
import functools

import jax
import jax.numpy as jnp
from jax import lax
from jax.experimental import pallas as pl
from jax.experimental.pallas import tpu as pltpu
from jax.sharding import PartitionSpec as P

PCOLS = 16
ITERS = 8
REACH = 3
RIM = 8

MESH = pl.DeviceIdType.MESH


def rows_up(extent):
    return extent // 2 + 1


def chunk_sizes(extent):
    size = max(6, extent // 10)
    full = extent // 2 // size - 1
    sent = rows_up(extent)
    up = [size] * full + [sent - size * full - 4, 4]
    down = [size] * full + [extent - sent - REACH - 1 - size * full, 2 * REACH]
    return up, down


def build_shifted(dst, local, temp, base, low, high, row_shift, col_shift):
    extent = local.shape[0]
    row_shift = jnp.broadcast_to(row_shift, (extent, row_shift.shape[1]))
    col_shift = jnp.broadcast_to(col_shift, (extent, col_shift.shape[1]))

    def row(i, carry):
        total = None
        for k in range(-REACH, REACH + 1):
            at = base + i + k
            value = local[lax.rem(at + extent, extent)].astype(jnp.float32)
            if low > 0:
                value = value * jnp.where((at >= low) & (at < high), 1.0, 0.0)
            total = value if total is None else jnp.where(row_shift == k, value, total)
        temp[pl.ds(RIM, extent), :] = total
        temp[pl.ds(0, RIM), :] = total[extent - RIM :]
        temp[pl.ds(RIM + extent, RIM), :] = total[:RIM]
        total = None
        for k in range(-REACH, REACH + 1):
            value = temp[pl.ds(RIM + k, extent), :]
            total = value if total is None else jnp.where(col_shift == k, value, total)
        dst[i, pl.ds(RIM, extent), :] = total
        dst[i, pl.ds(0, RIM), :] = total[extent - RIM :]
        dst[i, pl.ds(RIM + extent, RIM), :] = total[:RIM]
        return carry

    lax.fori_loop(0, dst.shape[0], row, 0)


def add_lags(sums, other, start, shifted, first, count):
    extent, lanes = other.shape[1:]

    def row(i, totals):
        value = other[start + i].astype(jnp.float32)
        result = []
        for a in range(3):
            for b in range(3):
                product = value * shifted[first + i + a, pl.ds(RIM + b - 1, extent), :]
                total = totals[3 * a + b]
                for j in range(extent // 8):
                    total = total + product[8 * j : 8 * j + 8]
                result.append(total)
        return tuple(result)

    begun = tuple(sums[k] for k in range(9))
    for k, total in enumerate(lax.fori_loop(0, count, row, begun)):
        sums[k] = total


def slot_places(extent_lanes, lanes, cols, patch_cols, homes):
    slot = lax.broadcasted_iota(jnp.int32, (2 * lanes, extent_lanes), 0)
    lane = lax.broadcasted_iota(jnp.int32, (2 * lanes, extent_lanes), 1)
    within = slot % patch_cols
    column = jnp.where(slot < lanes, within, jnp.where(within == 0, patch_cols, -1))
    return jnp.where(column == homes(lane), 1.0, 0.0).astype(jnp.bfloat16)


def by_patch_row(line, patch_rows):
    shape = (patch_rows, line.shape[1])
    slots = patch_rows * PCOLS
    of = lax.broadcasted_iota(jnp.int32, shape, 1) % slots // PCOLS
    return jnp.where(of == lax.broadcasted_iota(jnp.int32, shape, 0), line, 0.0)


def flow_lines(scores, row_shift, col_shift, live):
    weights = [score * score for score in scores]
    total = 1.0 + sum(weights)
    row_part = (weights[6] + weights[7] + weights[8] - weights[0] - weights[1] - weights[2]) / total
    col_part = (weights[2] + weights[5] + weights[8] - weights[0] - weights[3] - weights[6]) / total
    return (
        jnp.where(live > 0.0, row_shift + row_part, 0.0),
        jnp.where(live > 0.0, col_shift + col_part, 0.0),
    )


def kernel(
    sections, tiles,
    patch_ref, count_ref, shift_ref, prior_ref,
    line_ref, base_ref,
    local, merged, from_above, from_below, shifted_up, shifted_down, shifted_rim, temp, sums,
    count, shift, far_shift, prior, rims, far_rims, fields, goals, gain,
    info, east_info, part_up, part_down, own_up, east_up, east_down,
    local_sem, up_send, up_recv, down_send, down_recv,
    shift_sem, rim_sem, info_sem, part_sem, relay_sem, ready,
):
    sec, tile = lax.axis_index("sec"), lax.axis_index("tile")
    extent, lanes = local.shape[1:]
    sent = rows_up(extent)
    rim = 2 * REACH
    low = sent + REACH - 1
    up_sizes, down_sizes = chunk_sizes(extent)
    rows, cols = prior.shape[1:]
    patch_rows = lanes // PCOLS
    row_step, col_step = rows // patch_rows, cols // PCOLS
    has_below, has_above = sec > 0, sec < sections - 1
    has_west, has_east = tile > 0, tile < tiles - 1
    even = lax.rem(tile, 2) == 0
    middle, relay = sections // 2, len(up_sizes) - 2
    is_low, is_high = sec == middle - 1, sec == middle
    is_first, is_last = sec == 0, sec == sections - 1
    late_up, late_down = ~even & ~is_low, ~even & ~is_high
    own_pace = is_low | is_last

    far_rims[...] = jnp.zeros_like(far_rims)
    line_ref[...] = jnp.zeros_like(line_ref)
    for buffer in (info, east_info, part_up, part_down, own_up, east_up, east_down):
        buffer[...] = jnp.zeros_like(buffer)

    barrier = pltpu.get_barrier_semaphore()
    below, above = {"sec": sec - 1}, {"sec": sec + 1}
    west, east = {"tile": tile - 1}, {"tile": tile + 1}
    below_west = {"sec": sec - 1, "tile": tile - 1}
    partners = [
        (has_below, below),
        (has_above, above),
        (has_west, west),
        (has_east, east),
        (is_first, {"sec": middle}),
        (is_last, {"sec": middle}),
    ]
    partners[0] = (has_below & ~is_high, below)
    greeted = [has_below, has_above & ~is_low, has_west, has_east, is_high, is_high]

    def greet(where):
        return lambda: pl.semaphore_signal(
            barrier, 1, device_id=where, device_id_type=MESH
        )

    for have, where in partners:
        pl.when(have)(greet(where))
    waits = sum(jnp.where(have, 1, 0) for have in greeted)
    mine = [
        pltpu.make_async_copy(src, dst, local_sem.at[k])
        for k, (src, dst) in enumerate(
            ((shift_ref, shift), (count_ref, count), (prior_ref, prior), (patch_ref, local))
        )
    ]
    for copy in mine:
        copy.start()
    pl.semaphore_wait(barrier, waits)

    def remote(src, dst, sems, k, where):
        return pltpu.make_async_remote_copy(
            src_ref=src,
            dst_ref=dst,
            send_sem=sems[0].at[k],
            recv_sem=sems[1].at[k],
            device_id=where,
            device_id_type=MESH,
        )

    def remote_at(src, dst, sems, k, where):
        send, recv = sems.at[2 * k], sems.at[2 * k + 1]
        return pltpu.make_async_remote_copy(
            src_ref=src, dst_ref=dst, send_sem=send, recv_sem=recv, device_id=where, device_id_type=MESH
        )

    shift_copy = remote_at(shift_ref, far_shift, shift_sem, 0, above)
    pl.when(has_above & ~is_low)(shift_copy.start)
    ups, downs = [], []
    at = 0
    for c, size in enumerate(up_sizes):
        part = pl.ds(at, size)
        ups.append(remote(patch_ref.at[part], from_below.at[part], (up_send, up_recv), c, above))
        at += size
    at = 0
    for c, size in enumerate(down_sizes):
        part = pl.ds(at, size)
        source = merged if c == len(down_sizes) - 1 else patch_ref.at[pl.ds(low + at, size)]
        downs.append(remote(source, from_above.at[part], (down_send, down_recv), c, below))
        at += size
    held_up, held_down = pl.ds(0, up_sizes[relay]), pl.ds(0, down_sizes[relay])
    up_source = pl.ds(sum(up_sizes[:relay]), up_sizes[relay])
    down_offset = sum(down_sizes[:relay])
    up_leg = remote_at(
        patch_ref.at[up_source], from_above.at[held_up], relay_sem, 0, {"sec": sections - 1}
    )
    down_leg = remote_at(
        patch_ref.at[pl.ds(low + down_offset, down_sizes[relay])],
        from_below.at[held_down],
        relay_sem,
        1,
        {"sec": 0},
    )
    up_on = remote(
        from_above.at[held_up], from_below.at[up_source], (up_send, up_recv), relay, {"sec": middle}
    )
    down_on = remote(
        from_below.at[held_down],
        from_above.at[pl.ds(down_offset, down_sizes[relay])],
        (down_send, down_recv),
        relay,
        {"sec": middle - 1},
    )
    pl.when(is_high)(down_leg.start)
    for c in range(len(up_sizes)):
        sends_up = has_above & ~is_low & ~late_up if c >= relay else has_above & ~is_low
        pl.when(sends_up)(ups[c].start)
        if c < len(down_sizes) - 1:
            pl.when(has_below & ~is_high if c == relay else has_below)(downs[c].start)

    mine[0].wait()
    mine[1].wait()
    alive = jnp.where(
        lax.broadcasted_iota(jnp.int32, (1, lanes), 1) < count[0, 0], 1.0, 0.0
    )
    row_shift = shift[0:1, :].astype(jnp.float32)
    col_shift = shift[1:2, :].astype(jnp.float32)
    info[0:1, :] = row_shift
    info[1:2, :] = col_shift
    info[2:3, :] = alive
    mine[2].wait()
    for k in range(2):
        turned = jnp.transpose(prior[k])
        rims[0, k] = turned[:ITERS]
        rims[1, k] = turned[cols - ITERS :]
    info_copy = remote_at(info, east_info, info_sem, 0, west)
    pl.when(has_west)(info_copy.start)
    to_east = remote_at(rims.at[1], far_rims.at[1], rim_sem, 0, east)
    to_west = remote_at(rims.at[0], far_rims.at[0], rim_sem, 1, west)
    pl.when(has_east)(to_east.start)
    pl.when(has_west)(to_west.start)

    @pl.when(is_high)
    def _():
        pl.semaphore_signal(ready, 1, device_id=below, device_id_type=MESH)

    @pl.when(is_low)
    def _():
        pl.semaphore_wait(ready, 1)
        shift_copy.start()
        up_leg.start()
        for c in range(len(up_sizes)):
            if c != relay:
                ups[c].start()

    sums[...] = jnp.zeros_like(sums)
    mine[3].wait()

    @pl.when(has_below)
    def _():
        shift_copy.wait_recv()
        for j in range(rim):
            merged[j] = jnp.where(
                jnp.broadcast_to(far_shift[0:1, :], (extent, lanes)) <= j - REACH,
                local[sent - REACH - 1 + j].astype(jnp.float32),
                local[(extent - REACH + 1 + j) % extent].astype(jnp.float32),
            ).astype(jnp.bfloat16)
        build_shifted(
            shifted_up, local, temp, -1, 0, extent, far_shift[0:1, :], far_shift[1:2, :]
        )
        pl.when(~late_down)(downs[-1].start)

    @pl.when(has_above)
    def _():
        build_shifted(
            shifted_down, local, temp, sent - REACH - 2, sent, extent, -shift[0:1, :], -shift[1:2, :]
        )
        for i in range(rim + 2):
            shifted_rim[i] = shifted_down[i] + shifted_down[extent - sent + 2 + i]

    pl.when(has_west)(to_east.wait_recv)
    pl.when(has_east)(to_west.wait_recv)
    pl.when(has_east)(info_copy.wait_recv)
    lane = lax.broadcasted_iota(jnp.int32, (rows, cols), 1)
    in_east = (lane < ITERS) & has_east
    in_west = (lane >= cols - ITERS) & has_west
    for k in range(2):
        fields[k, :, :cols] = prior[k]
        between = jnp.zeros((cols - 2 * ITERS, rows), jnp.float32)
        fields[k, :, cols:] = jnp.transpose(
            jnp.concatenate([far_rims[0, k], between, far_rims[1, k]], 0)
        )
        fields[2 + k] = jnp.zeros((rows, 2 * cols), jnp.float32)
    inside = jnp.concatenate(
        [jnp.ones((rows, cols), jnp.float32), jnp.where(in_east | in_west, 1.0, 0.0)], 1
    )
    at_nodes = slot_places(
        2 * cols, lanes, cols, PCOLS,
        lambda lane: jnp.where(lane % col_step == 0, lane // col_step, -2),
    )
    both_alive = jnp.concatenate([alive, east_info[2:3, :]], 1)
    spots = jnp.dot(
        by_patch_row(both_alive, patch_rows).astype(jnp.bfloat16),
        at_nodes,
        preferred_element_type=jnp.float32,
    ).astype(jnp.bfloat16)
    spread = jnp.where(
        lax.broadcasted_iota(jnp.int32, (rows, patch_rows), 0)
        == row_step * lax.broadcasted_iota(jnp.int32, (rows, patch_rows), 1),
        1.0,
        0.0,
    ).astype(jnp.bfloat16)
    weight = jnp.dot(spread, spots, preferred_element_type=jnp.float32)
    gain[...] = (0.2 - 0.1 * weight) * inside
    wide_lane = lax.broadcasted_iota(jnp.int32, weight.shape, 1)
    for k in range(2):
        goals[k] = jnp.where(wide_lane // col_step % 2 == k, 0.4 * weight, 0.0)
    row = lax.broadcasted_iota(jnp.int32, weight.shape, 0)

    def sweep(_, carry):
        for k in range(4):
            field = fields[k]
            upper = jnp.where(row == 0, 0.0, pltpu.roll(field, 1, 0))
            lower = jnp.where(row == rows - 1, 0.0, pltpu.roll(field, rows - 1, 0))
            left = pltpu.roll(field, 1, 1)
            right = pltpu.roll(field, 2 * cols - 1, 1)
            field = 0.2 * field + gain[...] * ((upper + lower) + (left + right))
            fields[k] = field + goals[k - 2] if k >= 2 else field
        return carry

    lax.fori_loop(0, ITERS, sweep, 0)
    for k in range(4):
        base_ref[k] = fields[k, :, :cols]
    @pl.when(is_first)
    def _():
        down_leg.wait_recv()
        down_on.start()

    @pl.when(is_last)
    def _():
        up_leg.wait_recv()
        up_on.start()

    up_part = remote_at(part_up, own_up, part_sem, 0, below)
    up_part_west = remote_at(part_up, east_up, part_sem, 1, below_west)

    def take_up(c):
        at, size = sum(up_sizes[:c]), up_sizes[c]

        @pl.when(has_below)
        def _():
            ups[c].wait_recv()
            add_lags(sums.at[0], from_below, at, shifted_up, at, size)

    def take_down(c):
        at, size = sum(down_sizes[:c]), down_sizes[c]
        pl.when(has_above)(downs[c].wait_recv)
        if c == relay:
            pl.when(late_down & ~own_pace & has_below)(downs[-1].start)

        @pl.when(has_above)
        def _():
            if c == len(down_sizes) - 1:
                add_lags(sums.at[1], from_above, at, shifted_rim, 0, size)
            else:
                add_lags(sums.at[1], from_above, at, shifted_down, at + rim, size)

    for c in range(relay):
        take_up(c)
        take_down(c)
    pl.when(has_above & late_up)(ups[relay].start)
    pl.when(has_above & late_up)(ups[-1].start)
    take_down(relay)

    @pl.when(late_down & own_pace)
    def _():
        downs[relay].wait_send()
        downs[-1].start()

    take_up(relay)
    take_up(relay + 1)

    @pl.when(has_below)
    def _():
        for k in range(9):
            part_up[k : k + 1, :] = jnp.sum(sums[0, k], axis=0, keepdims=True)

    pl.when(has_below & has_west)(up_part_west.start)
    pl.when(has_below)(up_part.start)
    take_down(relay + 1)

    for k in range(9):
        part_down[k : k + 1, :] = jnp.sum(sums[1, 8 - k], axis=0, keepdims=True)
    down_part = remote_at(part_down, east_down, part_sem, 2, west)
    pl.when(has_west)(down_part.start)

    pl.when(has_above)(up_part.wait_recv)
    scale = float(extent)
    flow_a, flow_b = flow_lines(
        [(part_down[k : k + 1, :] + own_up[k : k + 1, :]) / scale for k in range(9)],
        row_shift,
        col_shift,
        alive,
    )
    line_ref[0:1, :] = flow_a
    line_ref[1:2, :] = flow_b
    pl.when(has_east)(down_part.wait_recv)
    pl.when(has_above & has_east)(up_part_west.wait_recv)
    east_a, east_b = flow_lines(
        [(east_down[k : k + 1, :] + east_up[k : k + 1, :]) / scale for k in range(9)],
        east_info[0:1, :],
        east_info[1:2, :],
        east_info[2:3, :],
    )
    line_ref[2:3, :] = east_a
    line_ref[3:4, :] = east_b

    pl.when(has_above)(shift_copy.wait_send)
    for c in range(len(up_sizes)):
        pl.when(has_above & ~is_low if c == relay else has_above)(ups[c].wait_send)
        sent_down = has_below & ~is_high & ~(late_down & own_pace) if c == relay else has_below
        pl.when(sent_down)(downs[c].wait_send)
    pl.when(is_low)(up_leg.wait_send)
    pl.when(is_high)(down_leg.wait_send)
    pl.when(is_first)(down_on.wait_send)
    pl.when(is_last)(up_on.wait_send)
    pl.when(has_east)(to_east.wait_send)
    pl.when(has_west)(to_west.wait_send)
    pl.when(has_west)(info_copy.wait_send)
    pl.when(has_below)(up_part.wait_send)
    pl.when(has_below & has_west)(up_part_west.wait_send)
    pl.when(has_west)(down_part.wait_send)


def finish_kernel(line_ref, base_ref, flow_ref, out_ref):
    rows, cols = base_ref.shape[1:]
    lanes = line_ref.shape[1]
    patch_rows, col_step = lanes // PCOLS, cols // PCOLS
    owners = slot_places(
        2 * cols, lanes, cols, PCOLS,
        lambda lane: jnp.where(
            lane < cols,
            2 * ((lane + col_step) // (2 * col_step)),
            2 * ((lane - cols) // (2 * col_step)) + 1,
        ),
    )

    step = rows // patch_rows
    flow_ref[...] = line_ref[0:2, :]
    left = jnp.concatenate(
        [
            by_patch_row(
                jnp.concatenate([line_ref[k : k + 1, :], line_ref[k + 2 : k + 3, :]], 1), patch_rows
            )
            for k in range(2)
        ],
        0,
    )
    first = left.astype(jnp.bfloat16)
    rest = left - first.astype(jnp.float32)
    second = rest.astype(jnp.bfloat16)
    third = (rest - second.astype(jnp.float32)).astype(jnp.bfloat16)
    parts = jnp.dot(
        jnp.concatenate([first, second, third], 0), owners, preferred_element_type=jnp.float32
    )
    size = 2 * patch_rows
    values = parts[:size] + parts[size : 2 * size] + parts[2 * size :]
    strip = step // 2
    for m in range(rows // strip):
        owner = (m + 1) // 2
        part = pl.ds(m * strip, strip)
        for k in range(2):
            result = base_ref[k, part, :]
            if owner < patch_rows:
                value = values[k * patch_rows + owner : k * patch_rows + owner + 1]
                result = (
                    result
                    + base_ref[2, part, :] * value[:, :cols]
                    + base_ref[3, part, :] * value[:, cols:]
                )
            out_ref[k, part, :] = result


def body(patches, counts, peak_shifts, mesh_prior):
    sections, tiles = lax.axis_size("sec"), lax.axis_size("tile")
    by_slot = jnp.transpose(patches[0], (1, 2, 0))
    extent, _, slots = by_slot.shape
    prior = mesh_prior[0, 0]
    rows, cols = prior.shape[1:]
    sent, rim = rows_up(extent), 2 * REACH
    up_sizes, down_sizes = chunk_sizes(extent)
    padded = extent + 2 * RIM
    sems = pltpu.SemaphoreType.DMA
    vmem = pl.BlockSpec(memory_space=pltpu.VMEM)
    f32, bf16 = jnp.float32, jnp.bfloat16
    lines, base = pl.pallas_call(
        functools.partial(kernel, sections, tiles),
        in_specs=[pl.BlockSpec(memory_space=pltpu.HBM)] * 4,
        out_specs=[vmem, vmem],
        out_shape=[
            pltpu.VMEM((8, slots), f32),
            pltpu.VMEM((4, rows, cols), f32),
        ],
        scratch_shapes=[
            pltpu.VMEM(by_slot.shape, bf16),
            pltpu.VMEM((rim, extent, slots), bf16),
            pltpu.VMEM((sum(down_sizes), extent, slots), bf16),
            pltpu.VMEM((sum(up_sizes), extent, slots), bf16),
            pltpu.VMEM((sent + 2, padded, slots), f32),
            pltpu.VMEM((extent - sent + 4 + rim, padded, slots), f32),
            pltpu.VMEM((rim + 2, padded, slots), f32),
            pltpu.VMEM((padded, slots), f32),
            pltpu.VMEM((2, 9, 8, slots), f32),
            pltpu.SMEM((1, 1), jnp.int32),
            pltpu.VMEM((2, slots), jnp.int32),
            pltpu.VMEM((2, slots), jnp.int32),
            pltpu.VMEM(prior.shape, f32),
            pltpu.VMEM((2, 2, ITERS, rows), f32),
            pltpu.VMEM((2, 2, ITERS, rows), f32),
            pltpu.VMEM((4, rows, 2 * cols), f32),
            pltpu.VMEM((2, rows, 2 * cols), f32),
            pltpu.VMEM((rows, 2 * cols), f32),
            pltpu.VMEM((8, slots), f32),
            pltpu.VMEM((8, slots), f32),
            pltpu.VMEM((16, slots), f32),
            pltpu.VMEM((16, slots), f32),
            pltpu.VMEM((16, slots), f32),
            pltpu.VMEM((16, slots), f32),
            pltpu.VMEM((16, slots), f32),
            sems((4,)),
            sems((len(up_sizes),)),
            sems((len(up_sizes),)),
            sems((len(down_sizes),)),
            sems((len(down_sizes),)),
            sems((2,)),
            sems((4,)),
            sems((2,)),
            sems((6,)),
            sems((4,)),
            pltpu.SemaphoreType.REGULAR,
        ],
        compiler_params=pltpu.CompilerParams(collective_id=0, has_side_effects=True),
    )(by_slot, counts, peak_shifts[0], prior)
    flows, displacement = pl.pallas_call(
        finish_kernel,
        in_specs=[vmem, vmem],
        out_specs=[vmem, vmem],
        out_shape=[
            jax.ShapeDtypeStruct((2, slots), f32),
            jax.ShapeDtypeStruct(prior.shape, f32),
        ],
    )(*[pltpu.with_memory_space_constraint(x, pltpu.VMEM) for x in (lines, base)])
    return flows[None], displacement[None, None]


def solution(mesh):
    placed = (
        P("sec", "tile", None, None),
        P("sec", "tile"),
        P("sec", None, "tile"),
        P("sec", "tile", None, None, None),
    )
    return jax.shard_map(
        body,
        mesh=mesh,
        in_specs=placed,
        out_specs=(P("sec", None, "tile"), P("sec", "tile", None, None, None)),
        check_vma=False,
    )
```
